256 devices in a mesh: gx: 8 (over z_hi, core), gy: 4 (over y), gz: 8 (over z_lo, x).
Axes of the slice: x: 4, y: 4, z: 8 (z_hi: 4, z_lo: 2; z = z_hi * 2 + z_lo), core: 2. Of those that a mesh axis runs over, the one named last changes fastest.
Arguments:
- features: bfloat16 [32768, 512], P(('gx', 'gy', 'gz')), may hold values from -6 to 6
- halo_index: int32 [24576], P(('gx', 'gy', 'gz')), may hold values from 0 to 127
- edge_src: int32 [2048, 384], P(('gx', 'gy', 'gz')), may hold values from 0 to 2623
- edge_dst: int32 [2048, 384], P(('gx', 'gy', 'gz')), may hold values from 0 to 127
- edge_count: int32 [2048], P(('gx', 'gy', 'gz')), may hold values from 48 to 384, as said below
- edge_basis: bfloat16 [786432, 128], P(('gx', 'gy', 'gz')), may hold values from -6 to 6
- w_edge_in: bfloat16 [8, 1152, 1024], P('gz'), may hold values from -0.1875 to 0.1875
- w_edge_out: bfloat16 [8, 1024, 512], P('gz'), may hold values from -0.1875 to 0.1875
- w_update: bfloat16 [512, 512], replicated, may hold values from -0.25 to 0.25
Outputs:
- new_features: bfloat16 [32768, 512], P(('gx', 'gy', 'gz'))
- halo_next: bfloat16 [6656, 96, 512], P(('gx', 'gy', 'gz'))
The draws below stay inside these ranges and needn't reach their ends.
Inputs may be any that keep to these rules, and one draw needn't show every extreme that they name: The first edge_count slots of a domain's 384 slots for a species pair are live; in every draw some species pair has all 384 slots live in every domain of one gz group.
All inputs are finite; a program needn't handle non-finite values.
Results may differ from the reference program's by a relative error of at most 0.0051.
Values may be sent and summed in bfloat16 or wider, within the bound.
No kernel may reach another device: no remote copies, remote signals or barrier semaphores. Data moves between devices by JAX's collectives and lax.ppermute only.
A program may use at most 128 MiB of HBM per device.

```python
import jax
import jax.numpy as jnp
from jax import lax

D = 512
HID = 1024
RB = 128
ATOM_DEV = 128
CAP = 384
HALO = 96
TABLE = 2624
TYPES = 8
ATOMS = 32768
N_GX = 8
N_GY = 4
N_GZ = 8
DEVICES = 256


def draw_edge_count(key, part):
    key_counts, key_group, key_helper = jax.random.split(key, 3)
    counts = jax.random.randint(key_counts, (DEVICES, N_GZ), CAP // 8, CAP + 1)
    group = jax.random.randint(key_group, (), 0, DEVICES // N_GZ)
    helper = jax.random.randint(key_helper, (), 0, N_GZ)
    rows = lax.broadcasted_iota(jnp.int32, (DEVICES, N_GZ), 0) // N_GZ
    columns = lax.broadcasted_iota(jnp.int32, (DEVICES, N_GZ), 1)
    filled = (rows == group) & (columns == helper)
    return jnp.where(filled, CAP, counts).reshape(DEVICES * N_GZ).astype(jnp.int32)


def set_ends(drawn, own_key, least, top_value):
    dims = drawn.shape
    spot = [jax.random.randint(jax.random.fold_in(own_key, axis), (), 0, dims[axis]) for axis in range(len(dims))]
    drawn = drawn.at[tuple(spot)].set(least)
    longest = dims.index(max(dims))
    spot[longest] = (spot[longest] + 1) % dims[longest]
    return drawn.at[tuple(spot)].set(top_value)


def levels(key, dims, cuts, smallest, top_value):
    def one(position, parts):
        draws = jax.random.uniform(jax.random.fold_in(jax.random.fold_in(key, 6), position), (parts,), jnp.float32, smallest / len(cuts), top_value / len(cuts))
        return jnp.repeat(jnp.exp(draws), dims[position] // parts).reshape((-1,) + (1,) * (len(dims) - position - 1))

    factor_of = one(*cuts[0])
    for cut in cuts[1:]:
        factor_of = factor_of * one(*cut)
    return factor_of


def normal_values(key, dims, width, reach, cuts=(), held_as=jnp.bfloat16):
    result = jax.random.normal(key, dims, jnp.float32) * width
    if len(cuts) > 0:
        result = levels(key, dims, cuts, -0.22, 0.18) * result
    return jnp.clip(result, min=-reach, max=reach).astype(held_as)


def setup_inputs(seed: int = 0) -> dict:
    key_of = jax.random.split(jax.random.key(seed), 10)
    features = normal_values(key_of[0], (ATOMS, D), 1.0, 6.0, ((0, 256),))
    halo_index = set_ends(jax.random.randint(key_of[1], (DEVICES * HALO,), 0, ATOM_DEV), jax.random.fold_in(key_of[1], 1), 0, ATOM_DEV - 1).astype(jnp.int32)
    edge_src = set_ends(jax.random.randint(key_of[2], (DEVICES * N_GZ, CAP), 0, TABLE), jax.random.fold_in(key_of[2], 1), 0, TABLE - 1).astype(jnp.int32)
    edge_dst = set_ends(jax.random.randint(key_of[3], (DEVICES * N_GZ, CAP), 0, ATOM_DEV), jax.random.fold_in(key_of[3], 1), 0, ATOM_DEV - 1).astype(jnp.int32)
    edge_count = draw_edge_count(jax.random.fold_in(key_of[9], 71), 0)
    edge_basis = normal_values(key_of[5], (DEVICES * N_GZ * CAP, RB), 1.0, 6.0, ((0, 256),))
    w_edge_in = normal_values(key_of[6], (TYPES, 2 * D + RB, HID), (2 * D + RB) ** -0.5, 0.1875, ((0, 8),))
    w_edge_out = normal_values(key_of[7], (TYPES, HID, D), HID ** -0.5, 0.1875, ((0, 8),))
    w_update = normal_values(key_of[8], (D, D), D ** -0.5, 0.25)
    return dict(features=features, halo_index=halo_index, edge_src=edge_src, edge_dst=edge_dst, edge_count=edge_count, edge_basis=edge_basis, w_edge_in=w_edge_in, w_edge_out=w_edge_out, w_update=w_update)


def neighbour_blocks(values, halo_index):
    boundary = jnp.take_along_axis(values, halo_index.reshape(DEVICES, HALO)[:, :, None], axis=1)
    boundary = boundary.reshape(N_GX, N_GY, N_GZ, HALO, D)
    blocks = []
    for shift_x in range(3):
        for shift_y in range(3):
            for shift_z in range(3):
                if shift_x == 1 and shift_y == 1 and (shift_z == 1):
                    continue
                blocks.append(jnp.roll(boundary, (1 - shift_x, 1 - shift_y, 1 - shift_z), axis=(0, 1, 2)))
    return jnp.stack(blocks, axis=3).reshape(DEVICES, 26 * HALO, D)

def reference(features, halo_index, edge_src, edge_dst, edge_count, edge_basis, w_edge_in, w_edge_out, w_update):
    own_rows = features.reshape(DEVICES, ATOM_DEV, D)
    table = jnp.concatenate([own_rows, neighbour_blocks(own_rows, halo_index)], axis=1)
    first_layer = w_edge_in.astype(jnp.float32)
    second_layer = w_edge_out.astype(jnp.float32)
    sources = edge_src.reshape(DEVICES, N_GZ, CAP)
    targets = edge_dst.reshape(DEVICES, N_GZ, CAP)
    counts = edge_count.reshape(DEVICES, N_GZ)
    basis = edge_basis.reshape(DEVICES, N_GZ, CAP, RB)

    def one_domain(items):
        table_rows, src_rows, dst_rows, count_rows, basis_rows = items
        inputs = jnp.concatenate([table_rows[src_rows], table_rows[dst_rows], basis_rows], axis=-1).astype(jnp.float32)
        pre = jnp.einsum('jck,jkh->jch', inputs, first_layer)
        hidden = lax.optimization_barrier(jax.nn.silu(pre).astype(jnp.bfloat16)).astype(jnp.float32)
        message = jnp.einsum('jch,jhd->jcd', hidden, second_layer).astype(jnp.bfloat16)
        message = lax.optimization_barrier(message).astype(jnp.float32)
        live = jnp.arange(CAP, dtype=jnp.int32)[None, :] < count_rows[:, None]
        message = jnp.where(live[:, :, None], message, jnp.float32(0.0))
        return jax.ops.segment_sum(message.reshape(-1, D), dst_rows.reshape(-1), num_segments=ATOM_DEV)
    aggregate = lax.map(one_domain, (table, sources, targets, counts, basis))
    normed = aggregate * lax.rsqrt(lax.optimization_barrier(jnp.mean(aggregate * aggregate, axis=-1, keepdims=True)) + 1e-05)
    normed = normed.astype(jnp.bfloat16).reshape(ATOMS, D)
    update = jnp.dot(normed, w_update, preferred_element_type=jnp.float32)
    new_features = (features.astype(jnp.float32) + update).astype(jnp.bfloat16)
    halo_next = neighbour_blocks(new_features.reshape(DEVICES, ATOM_DEV, D), halo_index)
    return (new_features, halo_next.reshape(DEVICES * 26, HALO, D))
```

```python
import functools

import jax
import jax.numpy as jnp
from jax import lax
from jax.experimental import pallas as pl
from jax.experimental.pallas import tpu as pltpu
from jax.sharding import PartitionSpec as P

PIECES = 9
VMEM_BYTES = 56 * 1024 * 1024


def ring(axis, step):
    count = lax.axis_size(axis)
    return [(i, (i + step) % count) for i in range(count)]


def from_before(x, axis):
    return lax.ppermute(x, axis, ring(axis, 1))


def from_after(x, axis):
    return lax.ppermute(x, axis, ring(axis, -1))


def inner_swap(x):
    count = lax.axis_size("gx")
    return lax.ppermute(x, "gx", [(i, i ^ 1) for i in range(count)])


def outer_swap(x):
    count = lax.axis_size("gx")
    pairs = [(i, (i + 1) % count if i % 2 else (i - 1) % count) for i in range(count)]
    return lax.ppermute(x, "gx", pairs)


def halo_pieces(block):
    own = jnp.stack([from_before(block, "gz"), block, from_after(block, "gz")])
    outer = outer_swap(own)
    before, after = from_before(own, "gy"), from_after(own, "gy")
    inner = inner_swap(own)
    outer_before, outer_after = from_before(outer, "gy"), from_after(outer, "gy")
    inner_before, inner_after = inner_swap(before), inner_swap(after)
    return (
        own, before, after,
        outer, outer_before, outer_after,
        inner, inner_before, inner_after,
    )


def table_row(edge_src, atom_count, halo_count, odd):
    outside = jnp.maximum(edge_src - atom_count, 0)
    k = outside // halo_count
    row = outside - k * halo_count
    cell = k + (k >= 13)
    a, b, c = cell // 9, (cell // 3) % 3, cell % 3
    column = jnp.where(a == 1, 0, jnp.where((a == 0) != odd, 1, 2))
    turn = jnp.where(b == 1, 0, jnp.where(b == 0, 1, 2))
    there = atom_count + ((column * 3 + turn) * 3 + c) * halo_count + row
    return jnp.where(edge_src < atom_count, edge_src, there)


def gather_kernel(index_ref, features_ref, *refs):
    pieces, (out_ref, table, picks, sems) = refs[:PIECES], refs[PIECES:]
    atoms = features_ref.shape[0]
    span = pieces[0].shape[0]
    used = atoms + PIECES * span
    slots = index_ref.shape[2]

    @pl.when(pl.program_id(0) == 0)
    def _():
        copies = [pltpu.make_async_copy(features_ref, table.at[pl.ds(0, atoms)], sems.at[0])]
        for n, piece in enumerate(pieces):
            where = table.at[pl.ds(atoms + n * span, span)]
            copies.append(pltpu.make_async_copy(piece, where, sems.at[n + 1]))
        for copy in copies:
            copy.start()
        table[pl.ds(used, table.shape[0] - used), :] = jnp.zeros(
            (table.shape[0] - used, table.shape[1]), table.dtype
        )
        for copy in copies:
            copy.wait()

    wide = lax.transpose(jnp.broadcast_to(index_ref[0], (128, slots)), (1, 0))
    lanes = lax.broadcasted_iota(jnp.int32, (slots, 128), 1)
    for n in range(table.shape[0] // 128):
        hit = wide == lanes + n * 128
        picks[:, n * 128 : (n + 1) * 128] = jnp.where(hit, 1.0, 0.0).astype(picks.dtype)
    out_ref[0] = jnp.dot(picks[...], table[...], preferred_element_type=jnp.float32).astype(
        out_ref.dtype
    )


def gather_rows(index, features, pieces):
    groups, slots = index.shape
    atoms, width = features.shape
    pieces = [piece.reshape(-1, width) for piece in pieces]
    rows = -(-(atoms + PIECES * pieces[0].shape[0]) // 256) * 256
    anywhere = pl.BlockSpec(memory_space=pl.ANY)
    return pl.pallas_call(
        gather_kernel,
        grid=(groups,),
        in_specs=[pl.BlockSpec((1, 1, slots), lambda g: (g, 0, 0))] + [anywhere] * (1 + PIECES),
        out_specs=pl.BlockSpec((1, slots, width), lambda g: (g, 0, 0)),
        out_shape=jax.ShapeDtypeStruct((groups, slots, width), features.dtype),
        scratch_shapes=[
            pltpu.VMEM((rows, width), features.dtype),
            pltpu.VMEM((slots, rows), features.dtype),
            pltpu.SemaphoreType.DMA((1 + PIECES,)),
        ],
        compiler_params=pltpu.CompilerParams(vmem_limit_bytes=VMEM_BYTES),
        cost_estimate=pl.CostEstimate(
            flops=2 * groups * slots * rows * width,
            bytes_accessed=2 * width * (rows + groups * slots),
            transcendentals=0,
        ),
        name="source_rows",
    )(index[:, None, :], features, *pieces)


def edge_kernel(first, last, source_ref, basis_ref, owner_ref, w_in_ref, w_out_ref, *refs):
    out_ref = refs[-1]
    slots, width = source_ref.shape[1:]
    atoms = out_ref.shape[1]
    target = owner_ref[0, atoms : atoms + 1, first : first + slots].astype(jnp.float32)
    atom = lax.broadcasted_iota(jnp.int32, (atoms, slots), 0).astype(jnp.float32)
    incidence = jnp.where(atom == target, 1.0, 0.0)
    target_rows = jnp.dot(
        lax.transpose(incidence, (1, 0)).astype(jnp.bfloat16),
        owner_ref[0, :atoms],
        preferred_element_type=jnp.float32,
    ).astype(jnp.bfloat16)
    pre = jnp.dot(source_ref[0], w_in_ref[:width], preferred_element_type=jnp.float32)
    pre += jnp.dot(target_rows, w_in_ref[width : 2 * width], preferred_element_type=jnp.float32)
    pre += jnp.dot(basis_ref[0], w_in_ref[2 * width :], preferred_element_type=jnp.float32)
    half = 0.5 * pre
    hidden = (half + half * jnp.tanh(half)).astype(jnp.bfloat16)
    message = jnp.dot(hidden, w_out_ref[...], preferred_element_type=jnp.float32)
    total = jnp.dot(
        incidence.astype(jnp.bfloat16),
        message.astype(jnp.bfloat16),
        preferred_element_type=jnp.float32,
    )
    if first:
        total += refs[0][0]
    out_ref[0] = total.astype(out_ref.dtype)


def edge_network(source, basis, owners, w_in, w_out, first, last, before):
    groups, slots, width = source.shape
    atoms = owners.shape[1] - 16
    hidden = w_out.shape[0]
    block = pl.BlockSpec((1, atoms, width), lambda g: (g, 0, 0))
    part = first // slots
    return pl.pallas_call(
        functools.partial(edge_kernel, first, last),
        grid=(groups,),
        in_specs=[
            pl.BlockSpec((1, slots, width), lambda g: (g, 0, 0)),
            pl.BlockSpec((1, slots, basis.shape[2]), lambda g: (g, part, 0)),
            pl.BlockSpec((1, owners.shape[1], width), lambda g: (g, 0, 0)),
            pl.BlockSpec(w_in.shape, lambda g: (0, 0)),
            pl.BlockSpec(w_out.shape, lambda g: (0, 0)),
        ]
        + [block] * len(before),
        out_specs=block,
        out_shape=jax.ShapeDtypeStruct(
            (groups, atoms, width), jnp.bfloat16 if last else jnp.float32
        ),
        compiler_params=pltpu.CompilerParams(vmem_limit_bytes=VMEM_BYTES),
        cost_estimate=pl.CostEstimate(
            flops=2 * groups * slots * hidden * (w_in.shape[0] + width),
            bytes_accessed=2 * (groups * slots * w_in.shape[0] + w_in.size + w_out.size),
            transcendentals=groups * slots * hidden,
        ),
        name="edge_network",
    )(source, basis, owners, w_in, w_out, *before)


def place_kernel(odd_ref, *refs):
    pieces, (out_ref, sems) = refs[:PIECES], refs[PIECES:]
    low = 17 * odd_ref[0]
    copies = []
    for n, piece in enumerate(pieces):
        column, turn = divmod(n, 3)
        b = (1, 0, 2)[turn]
        if n == 0:
            for c in (0, 2):
                copies.append((piece.at[pl.ds(c, 1)], out_ref.at[pl.ds(12 + c // 2, 1)]))
        else:
            if column == 0:
                start = 9 if b == 0 else 14
            else:
                start = 3 * b + (low if column == 1 else 17 - low)
            copies.append((piece, out_ref.at[pl.ds(start, 3)]))
    copies = [
        pltpu.make_async_copy(here, there, sems.at[i]) for i, (here, there) in enumerate(copies)
    ]
    for copy in copies:
        copy.start()
    for copy in copies:
        copy.wait()


def placed(pieces, odd):
    shape = pieces[0].shape
    anywhere = pl.BlockSpec(memory_space=pl.ANY)
    return pl.pallas_call(
        place_kernel,
        in_specs=[pl.BlockSpec(memory_space=pltpu.SMEM)] + [anywhere] * PIECES,
        out_specs=anywhere,
        out_shape=jax.ShapeDtypeStruct((26, *shape[1:]), pieces[0].dtype),
        scratch_shapes=[pltpu.SemaphoreType.DMA((PIECES + 1,))],
        name="place_blocks",
    )(odd.astype(jnp.int32)[None], *pieces)


def exchange(x):
    return lax.all_to_all(x, "gz", split_axis=0, concat_axis=0, tiled=True)


def shards(
    features,
    halo_index,
    edge_src,
    edge_dst,
    edge_count,
    edge_basis,
    w_edge_in,
    w_edge_out,
    w_update,
):
    atoms, width = features.shape
    groups, slots = edge_src.shape
    halo_count = halo_index.shape[0]
    odd = lax.axis_index("gx") % 2 == 1
    basis = exchange(edge_basis.reshape(groups, slots, -1))

    slot_index = lax.broadcasted_iota(jnp.int32, (groups, slots), 1)
    live = slot_index < edge_count[:, None]
    target = jnp.where(live, edge_dst, -1).astype(features.dtype)
    target = jnp.pad(target[:, None, :], ((0, 0), (0, 15), (0, width - slots)))
    copies = jnp.broadcast_to(features, (groups, atoms, width))
    owners = exchange(jnp.concatenate([copies, target], axis=1))

    pieces = halo_pieces(features[halo_index])
    index = table_row(edge_src, atoms, halo_count, odd)
    half = slots // 2
    source_0 = exchange(gather_rows(index[:, :half], features, pieces))
    source_1 = exchange(gather_rows(index[:, half:], features, pieces))
    network = functools.partial(
        edge_network, basis=basis, owners=owners, w_in=w_edge_in[0], w_out=w_edge_out[0]
    )
    partial_sums = network(source_0, first=0, last=False, before=())
    partial_sums = network(source_1, first=half, last=True, before=(partial_sums,))

    summed = jnp.sum(exchange(partial_sums).astype(jnp.float32), axis=0)
    mean_square = jnp.mean(summed * summed, axis=-1, keepdims=True)
    normed = (summed * lax.rsqrt(mean_square + 1e-05)).astype(jnp.bfloat16)
    update = jnp.dot(normed, w_update, preferred_element_type=jnp.float32)
    new_rows = (features.astype(jnp.float32) + update).astype(jnp.bfloat16)
    return new_rows, placed(halo_pieces(new_rows[halo_index]), odd)


def solution(mesh):
    everywhere = ("gx", "gy", "gz")
    in_specs = (
        P(everywhere, None),
        P(everywhere),
        P(everywhere, None),
        P(everywhere, None),
        P(everywhere),
        P(everywhere, None),
        P("gz", None, None),
        P("gz", None, None),
        P(),
    )
    out_specs = (P(everywhere, None), P(everywhere, None, None))
    return jax.shard_map(shards, mesh=mesh, in_specs=in_specs, out_specs=out_specs, check_vma=False)
```

```python
import jax
import jax.numpy as jnp
from jax import lax
from jax.experimental import pallas as pl
from jax.experimental.pallas import tpu as pltpu
from jax.sharding import PartitionSpec as P

PIECES = 9
VMEM_BYTES = 56 * 1024 * 1024


def ring(axis, step):
    count = lax.axis_size(axis)
    return [(i, (i + step) % count) for i in range(count)]


def from_before(x, axis):
    return lax.ppermute(x, axis, ring(axis, 1))


def from_after(x, axis):
    return lax.ppermute(x, axis, ring(axis, -1))


def inner_swap(x):
    count = lax.axis_size("gx")
    return lax.ppermute(x, "gx", [(i, i ^ 1) for i in range(count)])


def outer_swap(x):
    count = lax.axis_size("gx")
    pairs = [(i, (i + 1) % count if i % 2 else (i - 1) % count) for i in range(count)]
    return lax.ppermute(x, "gx", pairs)


def paired(place, count, side):
    return (place + (1 if place % 2 == side else -1)) % count


def device_permute(x, move):
    shape = [lax.axis_size(axis) for axis in ("gx", "gy", "gz")]
    along = shape[2] // 2
    pairs = []
    for source in range(shape[0] * shape[1] * shape[2]):
        gx, gy, gz = source // (shape[1] * shape[2]), source // shape[2] % shape[1], source % shape[2]
        there = move(gz % along, gy, gx // 2 * 2 + gz // along, gx % 2, along, shape[0])
        px, py, pz, core = there
        gx, gz = pz // 2 * 2 + core, pz % 2 * along + px
        pairs.append((source, (gx * shape[1] + py) * shape[2] + gz))
    return lax.ppermute(x, ("gx", "gy", "gz"), pairs)


def x_partner(x, y, z, core, count, depth):
    return paired(x, count, core), y, z, core


def z_partner(x, y, z, core, count, depth):
    return x, y, paired(z, depth, core), core


def far_partner(x, y, z, core, count, depth):
    return paired(x, count, core), y, paired(z, depth, core), core


def x_other(x, y, z, core, count, depth):
    return paired(x, count, 1 - core), y, z, core


def type_order():
    count = lax.axis_size("gz") // 2
    core, gz = lax.axis_index("gx") % 2, lax.axis_index("gz")
    x, low = gz % count, gz // count

    def beside(place, side):
        return (place + jnp.where(place % 2 == side, 1, -1)) % count

    here = [x, beside(x, 1 - core)]
    near = [beside(x, core), beside(beside(x, core), 1 - core)]
    up, down = low * count, (1 - low) * count
    return jnp.stack([up + t for t in here + near] + [down + t for t in here + near])


def halo_pieces(block):
    own = jnp.stack([from_before(block, "gz"), block, from_after(block, "gz")])
    outer = outer_swap(own)
    before, after = from_before(own, "gy"), from_after(own, "gy")
    inner = inner_swap(own)
    outer_before, outer_after = from_before(outer, "gy"), from_after(outer, "gy")
    inner_before, inner_after = inner_swap(before), inner_swap(after)
    return (
        own, before, after,
        outer, outer_before, outer_after,
        inner, inner_before, inner_after,
    )


def table_row(edge_src, atom_count, halo_count, odd):
    outside = jnp.maximum(edge_src - atom_count, 0)
    k = outside // halo_count
    row = outside - k * halo_count
    cell = k + (k >= 13)
    a, b, c = cell // 9, (cell // 3) % 3, cell % 3
    column = jnp.where(a == 1, 0, jnp.where((a == 0) != odd, 1, 2))
    turn = jnp.where(b == 1, 0, jnp.where(b == 0, 1, 2))
    there = atom_count + ((column * 3 + turn) * 3 + c) * halo_count + row
    return jnp.where(edge_src < atom_count, edge_src, there)


def gather_kernel(order_ref, index_ref, table_ref, *refs):
    basis_refs, (out_ref, picks) = refs[:2], refs[2:]
    slots = index_ref.shape[2]
    width = table_ref.shape[1]
    wide = lax.transpose(jnp.broadcast_to(index_ref[0], (128, slots)), (1, 0))
    lane = lax.broadcasted_iota(jnp.int32, (slots, 128), 1)
    spot = jnp.where((wide & 127) == lane, 1.0, 0.0).astype(jnp.bfloat16)
    tile = (wide >> 7).astype(jnp.float32).astype(jnp.bfloat16)
    for n in range(table_ref.shape[0] // 128):
        here = tile == jnp.full((), n, jnp.bfloat16)
        picks[:, n * 128 : (n + 1) * 128] = jnp.where(here, spot, jnp.zeros_like(spot))
    out_ref[0, :, :width] = jnp.dot(
        picks[...], table_ref[...], preferred_element_type=jnp.float32
    ).astype(out_ref.dtype)
    part = slots // 2
    for n, basis_ref in enumerate(basis_refs):
        out_ref[0, n * part : (n + 1) * part, width:] = basis_ref[0]


def gather_rows(order, index, table, basis):
    groups = index.shape[0] // 2
    slots = 2 * index.shape[1]
    rows, width = table.shape
    radial = basis.shape[2]
    return pl.pallas_call(
        gather_kernel,
        grid_spec=pltpu.PrefetchScalarGridSpec(
            num_scalar_prefetch=1,
            grid=(groups,),
            in_specs=[
                pl.BlockSpec((1, 1, slots), lambda g, order: (g, 0, 0)),
                pl.BlockSpec((rows, width), lambda g, order: (0, 0)),
                pl.BlockSpec((1, slots // 2, radial), lambda g, order: (order[2 * g], 0, 0)),
                pl.BlockSpec((1, slots // 2, radial), lambda g, order: (order[2 * g + 1], 0, 0)),
            ],
            out_specs=pl.BlockSpec((1, slots, width + radial), lambda g, order: (g, 0, 0)),
            scratch_shapes=[pltpu.VMEM((slots, rows), table.dtype)],
        ),
        out_shape=jax.ShapeDtypeStruct((groups, slots, width + radial), table.dtype),
        compiler_params=pltpu.CompilerParams(vmem_limit_bytes=VMEM_BYTES),
        cost_estimate=pl.CostEstimate(
            flops=2 * groups * slots * rows * width,
            bytes_accessed=2 * width * (rows + groups * slots),
            transcendentals=0,
        ),
        name="source_rows",
    )(order, index.reshape(groups, 1, slots), table, basis, basis)


def edge_kernel(rows_ref, owner_ref, in_0, out_0, in_1, out_1, sum_ref):
    atoms, width = sum_ref.shape
    slots = rows_ref.shape[1] // 2
    total = None
    for n, (w_in, w_out) in enumerate(((in_0, out_0), (in_1, out_1))):
        part = slice(n * slots, (n + 1) * slots)
        target = owner_ref[atoms + n : atoms + n + 1, :slots].astype(jnp.float32)
        atom = lax.broadcasted_iota(jnp.int32, (atoms, slots), 0).astype(jnp.float32)
        incidence = jnp.where(atom == target, 1.0, 0.0)
        target_rows = jnp.dot(
            lax.transpose(incidence, (1, 0)).astype(jnp.bfloat16),
            owner_ref[:atoms],
            preferred_element_type=jnp.float32,
        ).astype(jnp.bfloat16)
        pre = jnp.dot(rows_ref[0, part, :width], w_in[0, :width], preferred_element_type=jnp.float32)
        pre += jnp.dot(
            target_rows, w_in[0, width : 2 * width], preferred_element_type=jnp.float32
        )
        pre += jnp.dot(
            rows_ref[0, part, width:], w_in[0, 2 * width :], preferred_element_type=jnp.float32
        )
        half = 0.5 * pre
        hidden = (half + half * jnp.tanh(half)).astype(jnp.bfloat16)
        message = jnp.dot(hidden, w_out[0], preferred_element_type=jnp.float32)
        one = jnp.dot(
            incidence.astype(jnp.bfloat16),
            message.astype(jnp.bfloat16),
            preferred_element_type=jnp.float32,
        )
        total = one if total is None else total + one
    sum_ref[...] = total.astype(sum_ref.dtype)


def edge_network(rows, owner, networks, dtype):
    atoms, width = owner.shape[0] - 16, owner.shape[1]
    weights = [w for network in networks for w in network]
    slots = rows.shape[1]
    hidden = weights[1].shape[1]
    whole = pl.BlockSpec(memory_space=pltpu.VMEM)
    return pl.pallas_call(
        edge_kernel,
        in_specs=[whole] * 6,
        out_specs=whole,
        out_shape=jax.ShapeDtypeStruct((atoms, width), dtype),
        compiler_params=pltpu.CompilerParams(vmem_limit_bytes=VMEM_BYTES),
        cost_estimate=pl.CostEstimate(
            flops=2 * slots * hidden * (weights[0].shape[1] + width),
            bytes_accessed=2 * (rows.size + sum(w.size for w in weights)),
            transcendentals=slots * hidden,
        ),
        name="edge_network",
    )(rows, owner, *weights)


def place_kernel(odd_ref, *refs):
    pieces, (out_ref, sems) = refs[:PIECES], refs[PIECES:]
    low = 17 * odd_ref[0]
    copies = []
    for n, piece in enumerate(pieces):
        column, turn = divmod(n, 3)
        b = (1, 0, 2)[turn]
        if n == 0:
            for c in (0, 2):
                copies.append((piece.at[pl.ds(c, 1)], out_ref.at[pl.ds(12 + c // 2, 1)]))
        else:
            if column == 0:
                start = 9 if b == 0 else 14
            else:
                start = 3 * b + (low if column == 1 else 17 - low)
            copies.append((piece, out_ref.at[pl.ds(start, 3)]))
    copies = [
        pltpu.make_async_copy(here, there, sems.at[i]) for i, (here, there) in enumerate(copies)
    ]
    for copy in copies:
        copy.start()
    for copy in copies:
        copy.wait()


def placed(pieces, odd):
    shape = pieces[0].shape
    return pl.pallas_call(
        place_kernel,
        in_specs=[pl.BlockSpec(memory_space=pltpu.SMEM)]
        + [pl.BlockSpec(memory_space=pltpu.VMEM)] * PIECES,
        out_specs=pl.BlockSpec(memory_space=pl.ANY),
        out_shape=jax.ShapeDtypeStruct((26, *shape[1:]), pieces[0].dtype),
        scratch_shapes=[pltpu.SemaphoreType.DMA((PIECES + 1,))],
        compiler_params=pltpu.CompilerParams(vmem_limit_bytes=VMEM_BYTES),
        name="place_blocks",
    )(odd.astype(jnp.int32)[None], *pieces)


def shards(
    features,
    halo_index,
    edge_src,
    edge_dst,
    edge_count,
    edge_basis,
    w_edge_in,
    w_edge_out,
    w_update,
):
    atoms, width = features.shape
    groups, slots = edge_src.shape
    halo_count = halo_index.shape[0]
    odd = lax.axis_index("gx") % 2 == 1
    order = type_order()
    partners = (x_partner, z_partner, far_partner)

    pieces = halo_pieces(features[halo_index])
    mine = (w_edge_in, w_edge_out)
    other = tuple(device_permute(w, x_other) for w in mine)

    slot_index = lax.broadcasted_iota(jnp.int32, (groups, slots), 1)
    live = slot_index < edge_count[:, None]
    target = jnp.where(live, edge_dst, -1)[order].astype(features.dtype)
    target = jnp.pad(target.reshape(4, 2, slots), ((0, 0), (0, 14), (0, width - slots)))
    owned = [jnp.concatenate([features, target[n]], axis=0) for n in range(4)]
    owners = [device_permute(owned[n + 1], partner) for n, partner in enumerate(partners)]

    index = table_row(edge_src[order], atoms, halo_count, odd)
    rows = -(-(atoms + 27 * halo_count) // 256) * 256
    flat = [features] + [piece.reshape(-1, width) for piece in pieces]
    spare = jnp.zeros((rows - sum(part.shape[0] for part in flat), width), features.dtype)
    table = jnp.concatenate([*flat, spare], axis=0)
    basis = edge_basis.reshape(groups, slots, -1)

    def gathered(n):
        return gather_rows(order[2 * n : 2 * n + 2], index[2 * n : 2 * n + 2], table, basis)

    there = [device_permute(gathered(n + 1), partner) for n, partner in reversed(list(enumerate(partners)))][::-1]
    total = edge_network(gathered(0), owned[0], (mine, other), jnp.float32)
    for n, partner in enumerate(partners):
        answer = edge_network(there[n], owners[n], (mine, other), jnp.bfloat16)
        total += device_permute(answer, partner).astype(jnp.float32)

    mean_square = jnp.mean(total * total, axis=-1, keepdims=True)
    normed = (total * lax.rsqrt(mean_square + 1e-05)).astype(jnp.bfloat16)
    update = jnp.dot(normed, w_update, preferred_element_type=jnp.float32)
    new_rows = (features.astype(jnp.float32) + update).astype(jnp.bfloat16)
    return new_rows, placed(halo_pieces(new_rows[halo_index]), odd)


def solution(mesh):
    everywhere = ("gx", "gy", "gz")
    in_specs = (
        P(everywhere, None),
        P(everywhere),
        P(everywhere, None),
        P(everywhere, None),
        P(everywhere),
        P(everywhere, None),
        P("gz", None, None),
        P("gz", None, None),
        P(),
    )
    out_specs = (P(everywhere, None), P(everywhere, None, None))
    return jax.shard_map(shards, mesh=mesh, in_specs=in_specs, out_specs=out_specs, check_vma=False)
```

```python
import functools

import jax
import jax.numpy as jnp
from jax import lax
from jax.experimental import pallas as pl
from jax.experimental.pallas import tpu as pltpu
from jax.sharding import PartitionSpec as P

PIECES = 9
VMEM_BYTES = 24 * 1024 * 1024


def ring(axis, step):
    count = lax.axis_size(axis)
    return [(i, (i + step) % count) for i in range(count)]


def from_before(x, axis):
    return lax.ppermute(x, axis, ring(axis, 1))


def from_after(x, axis):
    return lax.ppermute(x, axis, ring(axis, -1))


def inner_swap(x):
    count = lax.axis_size("gx")
    return lax.ppermute(x, "gx", [(i, i ^ 1) for i in range(count)])


def outer_swap(x):
    count = lax.axis_size("gx")
    pairs = [(i, (i + 1) % count if i % 2 else (i - 1) % count) for i in range(count)]
    return lax.ppermute(x, "gx", pairs)


def paired(place, count, side):
    return (place + (1 if place % 2 == side else -1)) % count


def device_permute(x, move):
    shape = [lax.axis_size(axis) for axis in ("gx", "gy", "gz")]
    along = shape[2] // 2
    pairs = []
    for source in range(shape[0] * shape[1] * shape[2]):
        gx, gy, gz = source // (shape[1] * shape[2]), source // shape[2] % shape[1], source % shape[2]
        there = move(gz % along, gy, gx // 2 * 2 + gz // along, gx % 2, along, shape[0])
        px, py, pz, core = there
        gx, gz = pz // 2 * 2 + core, pz % 2 * along + px
        pairs.append((source, (gx * shape[1] + py) * shape[2] + gz))
    return lax.ppermute(x, ("gx", "gy", "gz"), pairs)


def x_partner(x, y, z, core, count, depth):
    return paired(x, count, core), y, z, core


def z_partner(x, y, z, core, count, depth):
    return x, y, paired(z, depth, core), core


def far_partner(x, y, z, core, count, depth):
    return paired(x, count, core), y, paired(z, depth, core), core


def x_other(x, y, z, core, count, depth):
    return paired(x, count, 1 - core), y, z, core


def type_order():
    count = lax.axis_size("gz") // 2
    core, gz = lax.axis_index("gx") % 2, lax.axis_index("gz")
    x, low = gz % count, gz // count

    def beside(place, side):
        return (place + jnp.where(place % 2 == side, 1, -1)) % count

    here = [x, beside(x, 1 - core)]
    near = [beside(x, core), beside(beside(x, core), 1 - core)]
    up, down = low * count, (1 - low) * count
    return jnp.stack([up + t for t in here + near] + [down + t for t in here + near])


def halo_pieces(block):
    own = jnp.stack([from_before(block, "gz"), block, from_after(block, "gz")])
    outer = outer_swap(own)
    before, after = from_before(own, "gy"), from_after(own, "gy")
    inner = inner_swap(own)
    outer_before, outer_after = from_before(outer, "gy"), from_after(outer, "gy")
    inner_before, inner_after = inner_swap(before), inner_swap(after)
    return (
        own, before, after,
        outer, outer_before, outer_after,
        inner, inner_before, inner_after,
    )


def whole_blocks(count):
    return [pl.BlockSpec(memory_space=pltpu.VMEM)] * count


def picked(index, rows):
    count = index.shape[1]
    wide = lax.transpose(jnp.broadcast_to(index, (rows, count)), (1, 0))
    lane = lax.broadcasted_iota(jnp.int32, (count, rows), 1)
    return jnp.where(wide == lane, 1.0, 0.0).astype(jnp.bfloat16)


def boundary_kernel(index_ref, rows_ref, out_ref):
    hit = picked(index_ref[...], rows_ref.shape[0])
    out_ref[...] = jnp.dot(hit, rows_ref[...], preferred_element_type=jnp.float32).astype(
        out_ref.dtype
    )


def boundary_of(index, rows):
    return pl.pallas_call(
        boundary_kernel,
        in_specs=whole_blocks(2),
        out_specs=pl.BlockSpec(memory_space=pltpu.VMEM),
        out_shape=jax.ShapeDtypeStruct((index.shape[1], rows.shape[1]), rows.dtype),
        compiler_params=pltpu.CompilerParams(vmem_limit_bytes=VMEM_BYTES),
        name="boundary",
    )(index, rows)


def owner_kernel(order_ref, count_ref, rows_ref, target_ref, *outs):
    atoms, width = rows_ref.shape
    slots = target_ref.shape[2]
    slot = lax.broadcasted_iota(jnp.int32, (1, slots), 1)
    line = lax.broadcasted_iota(jnp.int32, (16, slots), 0)
    for n, out_ref in enumerate(outs):
        out_ref[:atoms] = rows_ref[...]
        block = jnp.zeros((16, slots), jnp.float32)
        for t in range(2):
            j = order_ref[2 * n + t]
            target = jnp.where(slot < count_ref[j], target_ref[j], -1).astype(jnp.float32)
            block = jnp.where(line == t, target, block)
        out_ref[atoms:, :slots] = block.astype(out_ref.dtype)
        out_ref[atoms:, slots:] = jnp.zeros((16, width - slots), out_ref.dtype)


def owner_rows(order, count, rows, target):
    atoms, width = rows.shape
    shape = jax.ShapeDtypeStruct((atoms + 16, width), rows.dtype)
    return pl.pallas_call(
        owner_kernel,
        in_specs=[pl.BlockSpec(memory_space=pltpu.SMEM)] * 2 + whole_blocks(2),
        out_specs=whole_blocks(4),
        out_shape=[shape] * 4,
        compiler_params=pltpu.CompilerParams(vmem_limit_bytes=VMEM_BYTES),
        name="owner_rows",
    )(order, count, rows, target[:, None, :])


def table_kernel(*refs):
    parts, out_ref = refs[:-1], refs[-1]
    start = 0
    for part in parts:
        out_ref[start : start + part.shape[0]] = part[...]
        start += part.shape[0]
    out_ref[start:] = jnp.zeros((out_ref.shape[0] - start, out_ref.shape[1]), out_ref.dtype)


def table_of(parts):
    width = parts[0].shape[1]
    rows = -(-sum(part.shape[0] for part in parts) // 256) * 256
    return pl.pallas_call(
        table_kernel,
        in_specs=whole_blocks(len(parts)),
        out_specs=pl.BlockSpec(memory_space=pltpu.VMEM),
        out_shape=jax.ShapeDtypeStruct((rows, width), parts[0].dtype),
        compiler_params=pltpu.CompilerParams(vmem_limit_bytes=VMEM_BYTES),
        name="source_table",
    )(*parts)


def whole_part(value, divisor):
    return jnp.floor((value.astype(jnp.float32) + 0.5) * (1.0 / divisor)).astype(jnp.int32)


def table_row(source, atoms, halo_count, odd):
    outside = jnp.maximum(source - atoms, 0)
    k = whole_part(outside, halo_count)
    row = outside - k * halo_count
    cell = jnp.where(k >= 13, k + 1, k)
    a = whole_part(cell, 9)
    b = whole_part(cell, 3) - 3 * a
    c = cell - 9 * a - 3 * b
    column = jnp.where(a == 1, 0, jnp.where(a == 2 * odd, 1, 2))
    turn = jnp.where(b == 1, 0, jnp.where(b == 0, 1, 2))
    there = atoms + ((column * 3 + turn) * 3 + c) * halo_count + row
    return jnp.where(source < atoms, source, there)


def gather_kernel(atoms, halo_count, order_ref, source_ref, table_ref, basis_ref, out_ref, picks, sems):
    slots = source_ref.shape[2]
    width = table_ref.shape[1]
    copies = []
    for t in range(2):
        there = out_ref.at[pl.ds(t * slots, slots), pl.ds(width, out_ref.shape[1] - width)]
        copies.append(pltpu.make_async_copy(basis_ref.at[order_ref[t]], there, sems.at[t]))
    for copy in copies:
        copy.start()
    lane = lax.broadcasted_iota(jnp.int32, (slots, 128), 1)
    for t in range(2):
        row = table_row(source_ref[order_ref[t]], atoms, halo_count, order_ref[2])
        wide = lax.transpose(jnp.broadcast_to(row, (128, slots)), (1, 0))
        spot = jnp.where((wide & 127) == lane, 1.0, 0.0).astype(jnp.bfloat16)
        tile = (wide >> 7).astype(jnp.float32).astype(jnp.bfloat16)
        for n in range(table_ref.shape[0] // 128):
            here = tile == jnp.full((), n, jnp.bfloat16)
            picks[t * slots : (t + 1) * slots, n * 128 : (n + 1) * 128] = jnp.where(
                here, spot, jnp.zeros_like(spot)
            )
    out_ref[:, :width] = jnp.dot(
        picks[...], table_ref[...], preferred_element_type=jnp.float32
    ).astype(out_ref.dtype)
    for copy in copies:
        copy.wait()


def gather_rows(order, source, table, basis, atoms, halo_count):
    groups, slots = source.shape
    rows, width = table.shape
    radial = basis.shape[2]
    return pl.pallas_call(
        functools.partial(gather_kernel, atoms, halo_count),
        in_specs=[pl.BlockSpec(memory_space=pltpu.SMEM)]
        + whole_blocks(2)
        + [pl.BlockSpec(memory_space=pl.ANY)],
        out_specs=pl.BlockSpec(memory_space=pltpu.VMEM),
        out_shape=jax.ShapeDtypeStruct((2 * slots, width + radial), table.dtype),
        scratch_shapes=[pltpu.VMEM((2 * slots, rows), table.dtype), pltpu.SemaphoreType.DMA((2,))],
        compiler_params=pltpu.CompilerParams(vmem_limit_bytes=VMEM_BYTES),
        cost_estimate=pl.CostEstimate(
            flops=4 * slots * rows * width,
            bytes_accessed=2 * width * (rows + 2 * slots),
            transcendentals=0,
        ),
        name="source_rows",
    )(order, source[:, None, :], table, basis)


def edge_kernel(rows_ref, owner_ref, in_0, out_0, in_1, out_1, sum_ref, inputs):
    atoms, width = sum_ref.shape
    slots = rows_ref.shape[0] // 2
    total = None
    for n, (w_in, w_out) in enumerate(((in_0, out_0), (in_1, out_1))):
        part = slice(n * slots, (n + 1) * slots)
        target = owner_ref[atoms + n : atoms + n + 1, :slots].astype(jnp.float32)
        atom = lax.broadcasted_iota(jnp.int32, (atoms, slots), 0).astype(jnp.float32)
        incidence = jnp.where(atom == target, 1.0, 0.0)
        inputs[:, :width] = rows_ref[part, :width]
        inputs[:, width : 2 * width] = jnp.dot(
            lax.transpose(incidence, (1, 0)).astype(jnp.bfloat16),
            owner_ref[:atoms],
            preferred_element_type=jnp.float32,
        ).astype(jnp.bfloat16)
        inputs[:, 2 * width :] = rows_ref[part, width:]
        pre = jnp.dot(inputs[...], w_in[0], preferred_element_type=jnp.float32)
        half = 0.5 * pre
        hidden = (half + half * jnp.tanh(half)).astype(jnp.bfloat16)
        message = jnp.dot(hidden, w_out[0], preferred_element_type=jnp.float32)
        one = jnp.dot(
            incidence.astype(jnp.bfloat16),
            message.astype(jnp.bfloat16),
            preferred_element_type=jnp.float32,
        )
        total = one if total is None else total + one
    sum_ref[...] = total.astype(sum_ref.dtype)


def edge_network(rows, owner, networks, dtype):
    atoms, width = owner.shape[0] - 16, owner.shape[1]
    weights = [w for network in networks for w in network]
    slots = rows.shape[0]
    hidden = weights[1].shape[1]
    return pl.pallas_call(
        edge_kernel,
        in_specs=whole_blocks(6),
        out_specs=pl.BlockSpec(memory_space=pltpu.VMEM),
        out_shape=jax.ShapeDtypeStruct((atoms, width), dtype),
        scratch_shapes=[pltpu.VMEM((slots // 2, weights[0].shape[1]), rows.dtype)],
        compiler_params=pltpu.CompilerParams(vmem_limit_bytes=VMEM_BYTES),
        cost_estimate=pl.CostEstimate(
            flops=2 * slots * hidden * (weights[0].shape[1] + width),
            bytes_accessed=2 * (rows.size + sum(w.size for w in weights)),
            transcendentals=slots * hidden,
        ),
        name="edge_network",
    )(rows, owner, *weights)


def place_kernel(odd_ref, *refs):
    pieces, (out_ref, sems) = refs[:PIECES], refs[PIECES:]
    low = 17 * odd_ref[0]
    copies = []
    for n, piece in enumerate(pieces):
        column, turn = divmod(n, 3)
        b = (1, 0, 2)[turn]
        if n == 0:
            for c in (0, 2):
                copies.append((piece.at[pl.ds(c, 1)], out_ref.at[pl.ds(12 + c // 2, 1)]))
        else:
            if column == 0:
                start = 9 if b == 0 else 14
            else:
                start = 3 * b + (low if column == 1 else 17 - low)
            copies.append((piece, out_ref.at[pl.ds(start, 3)]))
    copies = [
        pltpu.make_async_copy(here, there, sems.at[i]) for i, (here, there) in enumerate(copies)
    ]
    for copy in copies:
        copy.start()
    for copy in copies:
        copy.wait()


def placed(pieces, odd):
    shape = pieces[0].shape
    return pl.pallas_call(
        place_kernel,
        in_specs=[pl.BlockSpec(memory_space=pltpu.SMEM)]
        + whole_blocks(PIECES),
        out_specs=pl.BlockSpec(memory_space=pl.ANY),
        out_shape=jax.ShapeDtypeStruct((26, *shape[1:]), pieces[0].dtype),
        scratch_shapes=[pltpu.SemaphoreType.DMA((PIECES + 1,))],
        compiler_params=pltpu.CompilerParams(vmem_limit_bytes=VMEM_BYTES),
        name="place_blocks",
    )(odd[None], *pieces)


def update_kernel(index_ref, rows_ref, weight_ref, own_ref, *refs):
    answers, (new_ref, edge_ref) = refs[:-2], refs[-2:]
    total = own_ref[...]
    for answer in answers:
        total += answer[...].astype(jnp.float32)
    mean_square = jnp.mean(total * total, axis=-1, keepdims=True)
    normed = (total * lax.rsqrt(mean_square + 1e-05)).astype(jnp.bfloat16)
    update = jnp.dot(normed, weight_ref[...], preferred_element_type=jnp.float32)
    new_rows = (rows_ref[...].astype(jnp.float32) + update).astype(new_ref.dtype)
    new_ref[...] = new_rows
    hit = picked(index_ref[...], new_rows.shape[0])
    edge_ref[...] = jnp.dot(hit, new_rows, preferred_element_type=jnp.float32).astype(
        edge_ref.dtype
    )


def updated(index, rows, weight, own, answers):
    return pl.pallas_call(
        update_kernel,
        in_specs=whole_blocks(4 + len(answers)),
        out_specs=whole_blocks(2),
        out_shape=[
            jax.ShapeDtypeStruct(rows.shape, rows.dtype),
            jax.ShapeDtypeStruct((index.shape[1], rows.shape[1]), rows.dtype),
        ],
        compiler_params=pltpu.CompilerParams(vmem_limit_bytes=VMEM_BYTES),
        name="update",
    )(index, rows, weight, own, *answers)


def shards(
    features,
    halo_index,
    edge_src,
    edge_dst,
    edge_count,
    edge_basis,
    w_edge_in,
    w_edge_out,
    w_update,
):
    atoms, width = features.shape
    groups, slots = edge_src.shape
    halo_count = halo_index.shape[0]
    halo_row = halo_index[None, :]
    odd = (lax.axis_index("gx") % 2).astype(jnp.int32)
    order = type_order()
    partners = (x_partner, z_partner, far_partner)

    pieces = halo_pieces(boundary_of(halo_row, features))
    mine = (w_edge_in, w_edge_out)
    other = tuple(device_permute(w, x_other) for w in mine)

    edge_dst, _ = lax.optimization_barrier((edge_dst, pieces[0]))
    owned = owner_rows(order, edge_count, features, edge_dst)
    owners = [device_permute(owned[n + 1], partner) for n, partner in enumerate(partners)]

    table = table_of([features] + [piece.reshape(-1, width) for piece in pieces])
    basis = edge_basis.reshape(groups, slots, -1)

    def gathered(n):
        which = jnp.stack([order[2 * n], order[2 * n + 1], odd])
        return gather_rows(which, edge_src, table, basis, atoms, halo_count)

    there = [device_permute(gathered(n + 1), partner) for n, partner in enumerate(partners)]
    own = edge_network(gathered(0), owned[0], (mine, other), jnp.float32)
    answers = []
    for n, partner in enumerate(partners):
        answer = edge_network(there[n], owners[n], (mine, other), jnp.bfloat16)
        answers.append(device_permute(answer, partner))

    new_rows, boundary = updated(halo_row, features, w_update, own, answers)
    return new_rows, placed(halo_pieces(boundary), odd)


def solution(mesh):
    everywhere = ("gx", "gy", "gz")
    in_specs = (
        P(everywhere, None),
        P(everywhere),
        P(everywhere, None),
        P(everywhere, None),
        P(everywhere),
        P(everywhere, None),
        P("gz", None, None),
        P("gz", None, None),
        P(),
    )
    out_specs = (P(everywhere, None), P(everywhere, None, None))
    return jax.shard_map(shards, mesh=mesh, in_specs=in_specs, out_specs=out_specs, check_vma=False)
```

```python
import functools

import jax
import jax.numpy as jnp
from jax import lax
from jax.experimental import pallas as pl
from jax.experimental.pallas import tpu as pltpu
from jax.sharding import PartitionSpec as P

PIECES = 9
VMEM_BYTES = 16 * 1024 * 1024
SMALL_BYTES = 6 * 1024 * 1024
HELD_BYTES = 8 * 1024 * 1024


def ring(axis, step):
    count = lax.axis_size(axis)
    return [(i, (i + step) % count) for i in range(count)]


def from_before(x, axis):
    return lax.ppermute(x, axis, ring(axis, 1))


def from_after(x, axis):
    return lax.ppermute(x, axis, ring(axis, -1))


def inner_swap(x):
    count = lax.axis_size("gx")
    return lax.ppermute(x, "gx", [(i, i ^ 1) for i in range(count)])


def outer_swap(x):
    count = lax.axis_size("gx")
    pairs = [(i, (i + 1) % count if i % 2 else (i - 1) % count) for i in range(count)]
    return lax.ppermute(x, "gx", pairs)


def paired(place, count, side):
    return (place + (1 if place % 2 == side else -1)) % count


def device_permute(x, move):
    shape = [lax.axis_size(axis) for axis in ("gx", "gy", "gz")]
    along = shape[2] // 2
    pairs = []
    for source in range(shape[0] * shape[1] * shape[2]):
        gx, gy, gz = source // (shape[1] * shape[2]), source // shape[2] % shape[1], source % shape[2]
        there = move(gz % along, gy, gx // 2 * 2 + gz // along, gx % 2, along, shape[0])
        px, py, pz, core = there
        gx, gz = pz // 2 * 2 + core, pz % 2 * along + px
        pairs.append((source, (gx * shape[1] + py) * shape[2] + gz))
    return lax.ppermute(x, ("gx", "gy", "gz"), pairs)


def x_partner(x, y, z, core, count, depth):
    return paired(x, count, core), y, z, core


def z_partner(x, y, z, core, count, depth):
    return x, y, paired(z, depth, core), core


def far_partner(x, y, z, core, count, depth):
    return paired(x, count, core), y, paired(z, depth, core), core


def x_other(x, y, z, core, count, depth):
    return paired(x, count, 1 - core), y, z, core


def type_order():
    count = lax.axis_size("gz") // 2
    core, gz = lax.axis_index("gx") % 2, lax.axis_index("gz")
    x, low = gz % count, gz // count

    def beside(place, side):
        return (place + jnp.where(place % 2 == side, 1, -1)) % count

    here = [x, beside(x, 1 - core)]
    near = [beside(x, core), beside(beside(x, core), 1 - core)]
    up, down = low * count, (1 - low) * count
    holders = ((up, here), (down, here), (up, near), (down, near))
    return jnp.stack([base + t for base, places in holders for t in places])


def halo_pieces(block):
    own = jnp.stack([from_before(block, "gz"), block, from_after(block, "gz")])
    outer = outer_swap(own)
    before, after = from_before(own, "gy"), from_after(own, "gy")
    inner = inner_swap(own)
    outer_before, outer_after = from_before(outer, "gy"), from_after(outer, "gy")
    inner_before, inner_after = inner_swap(before), inner_swap(after)
    return (
        own, before, after,
        outer, outer_before, outer_after,
        inner, inner_before, inner_after,
    )


def whole_blocks(count):
    return [pl.BlockSpec(memory_space=pltpu.VMEM)] * count


def picked(index, rows):
    count = index.shape[1]
    wide = lax.transpose(jnp.broadcast_to(index, (rows, count)), (1, 0))
    lane = lax.broadcasted_iota(jnp.int32, (count, rows), 1)
    return jnp.where(wide == lane, 1.0, 0.0).astype(jnp.bfloat16)


def boundary_kernel(index_ref, rows_ref, out_ref):
    hit = picked(index_ref[...], rows_ref.shape[0])
    out_ref[...] = jnp.dot(hit, rows_ref[...], preferred_element_type=jnp.float32).astype(
        out_ref.dtype
    )


def boundary_of(index, rows):
    return pl.pallas_call(
        boundary_kernel,
        in_specs=whole_blocks(2),
        out_specs=pl.BlockSpec(memory_space=pltpu.VMEM),
        out_shape=jax.ShapeDtypeStruct((index.shape[1], rows.shape[1]), rows.dtype),
        compiler_params=pltpu.CompilerParams(vmem_limit_bytes=SMALL_BYTES),
        name="boundary",
    )(index, rows)


def table_kernel(*refs):
    parts, (out_ref, sems) = refs[:-2], refs[-2:]
    start = 0
    copies = []
    for n, part in enumerate(parts):
        there = out_ref.at[pl.ds(start, part.shape[0])]
        copies.append(pltpu.make_async_copy(part, there, sems.at[n]))
        start += part.shape[0]
    for copy in copies:
        copy.start()
    out_ref[start:] = jnp.zeros((out_ref.shape[0] - start, out_ref.shape[1]), out_ref.dtype)
    for copy in copies:
        copy.wait()


def table_of(parts):
    width = parts[0].shape[1]
    rows = -(-sum(part.shape[0] for part in parts) // 256) * 256
    return pl.pallas_call(
        table_kernel,
        in_specs=[pl.BlockSpec(memory_space=pl.ANY)] * len(parts),
        out_specs=pl.BlockSpec(memory_space=pltpu.VMEM),
        out_shape=jax.ShapeDtypeStruct((rows, width), parts[0].dtype),
        scratch_shapes=[pltpu.SemaphoreType.DMA((len(parts),))],
        compiler_params=pltpu.CompilerParams(vmem_limit_bytes=SMALL_BYTES),
        name="source_table",
    )(*parts)


def whole_part(value, divisor):
    return jnp.floor((value.astype(jnp.float32) + 0.5) * (1.0 / divisor)).astype(jnp.int32)


def table_row(source, atoms, halo_count, odd):
    outside = jnp.maximum(source - atoms, 0)
    k = whole_part(outside, halo_count)
    row = outside - k * halo_count
    cell = jnp.where(k >= 13, k + 1, k)
    a = whole_part(cell, 9)
    b = whole_part(cell, 3) - 3 * a
    c = cell - 9 * a - 3 * b
    column = jnp.where(a == 1, 0, jnp.where(a == 2 * odd, 1, 2))
    turn = jnp.where(b == 1, 0, jnp.where(b == 0, 1, 2))
    there = atoms + ((column * 3 + turn) * 3 + c) * halo_count + row
    return jnp.where(source < atoms, source, there)


def gather_kernel(
    atoms, halo_count, order_ref, count_ref, source_ref, target_ref, table_ref, basis_ref, *refs
):
    out_ref, picks, sems = refs
    slots = source_ref.shape[1]
    width = table_ref.shape[1]
    copies = []
    for t in range(2):
        there = out_ref.at[pl.ds(t * slots, slots), pl.ds(width, out_ref.shape[1] - width)]
        copies.append(pltpu.make_async_copy(basis_ref.at[order_ref[t]], there, sems.at[t]))
    for copy in copies:
        copy.start()
    lane = lax.broadcasted_iota(jnp.int32, (slots, 128), 1)
    slot = lax.broadcasted_iota(jnp.int32, (1, slots), 1)
    line = lax.broadcasted_iota(jnp.int32, (16, slots), 0)
    ends = jnp.zeros((16, slots), jnp.float32)
    for t in range(2):
        j = order_ref[t]
        row = table_row(source_ref[pl.ds(j, 1)], atoms, halo_count, order_ref[2])
        wide = lax.transpose(jnp.broadcast_to(row, (128, slots)), (1, 0))
        spot = jnp.where((wide & 127) == lane, 1.0, 0.0).astype(jnp.bfloat16)
        tile = (wide >> 7).astype(jnp.float32).astype(jnp.bfloat16)
        for n in range(table_ref.shape[0] // 128):
            here = tile == jnp.full((), n, jnp.bfloat16)
            picks[t * slots : (t + 1) * slots, n * 128 : (n + 1) * 128] = jnp.where(
                here, spot, jnp.zeros_like(spot)
            )
        target = jnp.where(slot < count_ref[j], target_ref[pl.ds(j, 1)], -1)
        ends = jnp.where(line == t, target.astype(jnp.float32), ends)
    out_ref[: 2 * slots, :width] = jnp.dot(
        picks[...], table_ref[...], preferred_element_type=jnp.float32
    ).astype(out_ref.dtype)
    start = 2 * slots
    out_ref[start : start + atoms, :width] = table_ref[:atoms]
    out_ref[start : start + atoms, width:] = jnp.zeros(
        (atoms, out_ref.shape[1] - width), out_ref.dtype
    )
    out_ref[start + atoms :, :slots] = ends.astype(out_ref.dtype)
    out_ref[start + atoms :, slots:] = jnp.zeros((16, out_ref.shape[1] - slots), out_ref.dtype)
    for copy in copies:
        copy.wait()


def gather_rows(order, count, source, target, table, basis, atoms, halo_count):
    slots = source.shape[1]
    rows, width = table.shape
    radial = basis.shape[2]
    shape = (2 * slots + atoms + 16, width + radial)
    return pl.pallas_call(
        functools.partial(gather_kernel, atoms, halo_count),
        in_specs=[pl.BlockSpec(memory_space=pltpu.SMEM)] * 2
        + whole_blocks(3)
        + [pl.BlockSpec(memory_space=pl.ANY)],
        out_specs=pl.BlockSpec(memory_space=pltpu.VMEM),
        out_shape=jax.ShapeDtypeStruct(shape, table.dtype),
        scratch_shapes=[pltpu.VMEM((2 * slots, rows), table.dtype), pltpu.SemaphoreType.DMA((2,))],
        compiler_params=pltpu.CompilerParams(vmem_limit_bytes=VMEM_BYTES),
        cost_estimate=pl.CostEstimate(
            flops=4 * slots * rows * width,
            bytes_accessed=2 * width * (rows + 2 * slots),
            transcendentals=0,
        ),
        name="source_rows",
    )(order, count, source, target, table, basis)


def network_parts(w_in, w_out, packed):
    depth, hidden = w_in.shape
    width = w_out.shape[1]
    parts = []
    for n in range(hidden // width):
        columns = w_in.at[:, pl.ds(n * width, width)]
        parts.append((columns, packed.at[pl.ds(n * depth, depth)]))
    parts.append((w_out, packed.at[pl.ds(hidden // width * depth, hidden)]))
    return parts


def moved(pairs, sems):
    copies = [
        pltpu.make_async_copy(here, there, sems.at[n]) for n, (here, there) in enumerate(pairs)
    ]
    for copy in copies:
        copy.start()
    for copy in copies:
        copy.wait()


def pack_kernel(in_ref, out_ref, packed_ref, sems):
    moved(network_parts(in_ref.at[0], out_ref.at[0], packed_ref), sems)


def packed_network(w_in, w_out):
    width = w_out.shape[2]
    rows = w_in.shape[1] * (w_in.shape[2] // width) + w_out.shape[1]
    return pl.pallas_call(
        pack_kernel,
        in_specs=[pl.BlockSpec(memory_space=pl.ANY)] * 2,
        out_specs=pl.BlockSpec(memory_space=pl.ANY),
        out_shape=jax.ShapeDtypeStruct((rows, width), w_in.dtype),
        scratch_shapes=[pltpu.SemaphoreType.DMA((1 + w_in.shape[2] // width,))],
        compiler_params=pltpu.CompilerParams(vmem_limit_bytes=SMALL_BYTES),
        name="packed_network",
    )(w_in, w_out)


def hold_kernel(in_0, out_0, packed, in_ref, out_ref, sems):
    pairs = [(in_0.at[0], in_ref.at[0]), (out_0.at[0], out_ref.at[0])]
    pairs += [(b, a) for a, b in network_parts(in_ref.at[1], out_ref.at[1], packed)]
    moved(pairs, sems)


def held(mine, other):
    return pl.pallas_call(
        hold_kernel,
        in_specs=[pl.BlockSpec(memory_space=pl.ANY)] * 3,
        out_specs=whole_blocks(2),
        out_shape=[jax.ShapeDtypeStruct((2, *w.shape[1:]), w.dtype) for w in mine],
        scratch_shapes=[pltpu.SemaphoreType.DMA((8,))],
        compiler_params=pltpu.CompilerParams(vmem_limit_bytes=HELD_BYTES),
        name="held_networks",
    )(*mine, other)


def edge_kernel(rows_ref, w_in, w_out, sum_ref, inputs, total):
    atoms, width = sum_ref.shape
    slots = inputs.shape[0]
    total[...] = jnp.zeros_like(total)

    def one(n, carry):
        edges = pl.ds(pl.multiple_of(n * slots, slots), slots)
        ends = rows_ref[2 * slots + atoms :, :slots].astype(jnp.float32)
        target = jnp.where(n == 0, ends[0:1], ends[1:2])
        atom = lax.broadcasted_iota(jnp.int32, (atoms, slots), 0).astype(jnp.float32)
        incidence = jnp.where(atom == target, 1.0, 0.0)
        inputs[:, :width] = rows_ref[edges, :width]
        inputs[:, width : 2 * width] = jnp.dot(
            lax.transpose(incidence, (1, 0)).astype(jnp.bfloat16),
            rows_ref[2 * slots : 2 * slots + atoms, :width],
            preferred_element_type=jnp.float32,
        ).astype(jnp.bfloat16)
        inputs[:, 2 * width :] = rows_ref[edges, width:]
        pre = jnp.dot(inputs[...], w_in[n], preferred_element_type=jnp.float32)
        half = 0.5 * pre
        hidden = (half + half * jnp.tanh(half)).astype(jnp.bfloat16)
        message = jnp.dot(hidden, w_out[n], preferred_element_type=jnp.float32)
        total[...] += jnp.dot(
            incidence.astype(jnp.bfloat16),
            message.astype(jnp.bfloat16),
            preferred_element_type=jnp.float32,
        )
        return carry

    lax.fori_loop(0, 2, one, 0)
    sum_ref[...] = total[...].astype(sum_ref.dtype)


def edge_network(rows, atoms, weights, dtype):
    w_in, w_out = weights
    width, hidden = w_out.shape[2], w_out.shape[1]
    slots = (rows.shape[0] - 16 - atoms) // 2
    return pl.pallas_call(
        edge_kernel,
        in_specs=whole_blocks(3),
        out_specs=pl.BlockSpec(memory_space=pltpu.VMEM),
        out_shape=jax.ShapeDtypeStruct((atoms, width), dtype),
        scratch_shapes=[
            pltpu.VMEM((slots, w_in.shape[1]), rows.dtype),
            pltpu.VMEM((atoms, width), jnp.float32),
        ],
        compiler_params=pltpu.CompilerParams(vmem_limit_bytes=VMEM_BYTES),
        cost_estimate=pl.CostEstimate(
            flops=4 * slots * hidden * (w_in.shape[1] + width),
            bytes_accessed=2 * (rows.size + w_in.size + w_out.size),
            transcendentals=2 * slots * hidden,
        ),
        name="edge_network",
    )(rows, w_in, w_out)


def place_kernel(odd_ref, *refs):
    pieces, (out_ref, sems) = refs[:PIECES], refs[PIECES:]
    low = 17 * odd_ref[0]
    copies = []
    for n, piece in enumerate(pieces):
        column, turn = divmod(n, 3)
        b = (1, 0, 2)[turn]
        if n == 0:
            for c in (0, 2):
                copies.append((piece.at[pl.ds(c, 1)], out_ref.at[pl.ds(12 + c // 2, 1)]))
        else:
            if column == 0:
                start = 9 if b == 0 else 14
            else:
                start = 3 * b + (low if column == 1 else 17 - low)
            copies.append((piece, out_ref.at[pl.ds(start, 3)]))
    copies = [
        pltpu.make_async_copy(here, there, sems.at[i]) for i, (here, there) in enumerate(copies)
    ]
    for copy in copies:
        copy.start()
    for copy in copies:
        copy.wait()


def placed(pieces, odd):
    shape = pieces[0].shape
    return pl.pallas_call(
        place_kernel,
        in_specs=[pl.BlockSpec(memory_space=pltpu.SMEM)]
        + whole_blocks(PIECES),
        out_specs=pl.BlockSpec(memory_space=pl.ANY),
        out_shape=jax.ShapeDtypeStruct((26, *shape[1:]), pieces[0].dtype),
        scratch_shapes=[pltpu.SemaphoreType.DMA((10,))],
        compiler_params=pltpu.CompilerParams(vmem_limit_bytes=SMALL_BYTES),
        name="place_blocks",
    )(odd[None], *pieces)


def update_kernel(index_ref, rows_ref, weight_ref, own_ref, *refs):
    answers, (new_ref, edge_ref) = refs[:-2], refs[-2:]
    total = own_ref[...]
    for answer in answers:
        total += answer[...].astype(jnp.float32)
    mean_square = jnp.mean(total * total, axis=-1, keepdims=True)
    normed = (total * lax.rsqrt(mean_square + 1e-05)).astype(jnp.bfloat16)
    update = jnp.dot(normed, weight_ref[...], preferred_element_type=jnp.float32)
    new_rows = (rows_ref[...].astype(jnp.float32) + update).astype(new_ref.dtype)
    new_ref[...] = new_rows
    hit = picked(index_ref[...], new_rows.shape[0])
    edge_ref[...] = jnp.dot(hit, new_rows, preferred_element_type=jnp.float32).astype(
        edge_ref.dtype
    )


def updated(index, rows, weight, own, answers):
    return pl.pallas_call(
        update_kernel,
        in_specs=whole_blocks(4 + len(answers)),
        out_specs=whole_blocks(2),
        out_shape=[
            jax.ShapeDtypeStruct(rows.shape, rows.dtype),
            jax.ShapeDtypeStruct((index.shape[1], rows.shape[1]), rows.dtype),
        ],
        compiler_params=pltpu.CompilerParams(vmem_limit_bytes=SMALL_BYTES),
        name="update",
    )(index, rows, weight, own, *answers)


def shards(
    features,
    halo_index,
    edge_src,
    edge_dst,
    edge_count,
    edge_basis,
    w_edge_in,
    w_edge_out,
    w_update,
):
    atoms, width = features.shape
    groups, slots = edge_src.shape
    halo_count = halo_index.shape[0]
    halo_row = halo_index[None, :]
    odd = (lax.axis_index("gx") % 2).astype(jnp.int32)
    order = type_order()
    partners = (z_partner, x_partner, far_partner)

    pieces = halo_pieces(boundary_of(halo_row, features))
    mine = (w_edge_in, w_edge_out)
    packed, _ = lax.optimization_barrier((packed_network(*mine), pieces[0]))
    weights = held(mine, device_permute(packed, x_other))

    table = table_of([features] + [piece.reshape(-1, width) for piece in pieces])
    basis = edge_basis.reshape(groups, slots, -1)

    def gathered(n):
        which = jnp.stack([order[2 * n], order[2 * n + 1], odd])
        return gather_rows(
            which, edge_count, edge_src, edge_dst, table, basis, atoms, halo_count
        )

    there = [device_permute(gathered(n + 1), partner) for n, partner in enumerate(partners)]
    own = edge_network(gathered(0), atoms, weights, jnp.float32)
    answers = []
    for n, partner in enumerate(partners):
        answer = edge_network(there[n], atoms, weights, jnp.bfloat16)
        answers.append(device_permute(answer, partner))

    new_rows, boundary = updated(halo_row, features, w_update, own, answers)
    return new_rows, placed(halo_pieces(boundary), odd)


def solution(mesh):
    everywhere = ("gx", "gy", "gz")
    in_specs = (
        P(everywhere, None),
        P(everywhere),
        P(everywhere, None),
        P(everywhere, None),
        P(everywhere),
        P(everywhere, None),
        P("gz", None, None),
        P("gz", None, None),
        P(),
    )
    out_specs = (P(everywhere, None), P(everywhere, None, None))
    return jax.shard_map(shards, mesh=mesh, in_specs=in_specs, out_specs=out_specs, check_vma=False)
```

```python
import functools

import jax
import jax.numpy as jnp
from jax import lax
from jax.experimental import pallas as pl
from jax.experimental.pallas import tpu as pltpu
from jax.sharding import PartitionSpec as P

PIECES = 9
VMEM_BYTES = 12 * 1024 * 1024
GATHER_BYTES = 16 * 1024 * 1024
FIRST_BYTES = 14 * 1024 * 1024
SMALL_BYTES = 5 * 1024 * 1024


def ring(axis, step):
    count = lax.axis_size(axis)
    return [(i, (i + step) % count) for i in range(count)]


def from_before(x, axis):
    return lax.ppermute(x, axis, ring(axis, 1))


def from_after(x, axis):
    return lax.ppermute(x, axis, ring(axis, -1))


def inner_swap(x):
    count = lax.axis_size("gx")
    return lax.ppermute(x, "gx", [(i, i ^ 1) for i in range(count)])


def outer_swap(x):
    count = lax.axis_size("gx")
    pairs = [(i, (i + 1) % count if i % 2 else (i - 1) % count) for i in range(count)]
    return lax.ppermute(x, "gx", pairs)


def paired(place, count, side):
    return (place + (1 if place % 2 == side else -1)) % count


def device_permute(x, move):
    shape = [lax.axis_size(axis) for axis in ("gx", "gy", "gz")]
    along = shape[2] // 2
    pairs = []
    for source in range(shape[0] * shape[1] * shape[2]):
        gx, gy, gz = source // (shape[1] * shape[2]), source // shape[2] % shape[1], source % shape[2]
        there = move(gz % along, gy, gx // 2 * 2 + gz // along, gx % 2, along, shape[0])
        px, py, pz, core = there
        gx, gz = pz // 2 * 2 + core, pz % 2 * along + px
        pairs.append((source, (gx * shape[1] + py) * shape[2] + gz))
    return lax.ppermute(x, ("gx", "gy", "gz"), pairs)


def x_partner(x, y, z, core, count, depth):
    return paired(x, count, core), y, z, core


def z_partner(x, y, z, core, count, depth):
    return x, y, paired(z, depth, core), core


def far_partner(x, y, z, core, count, depth):
    return paired(x, count, core), y, paired(z, depth, core), core


def y_partner(x, y, z, core, count, depth):
    return x, paired(y, lax.axis_size("gy"), core), z, core


def x_other(x, y, z, core, count, depth):
    return paired(x, count, 1 - core), y, z, core


def type_order():
    count = lax.axis_size("gz") // 2
    core, gz = lax.axis_index("gx") % 2, lax.axis_index("gz")
    x, low = gz % count, gz // count

    def beside(place, side):
        return (place + jnp.where(place % 2 == side, 1, -1)) % count

    here = [x, beside(x, 1 - core)]
    near = [beside(x, core), beside(beside(x, core), 1 - core)]
    up, down = low * count, (1 - low) * count
    holders = ((up, here), (down, here), (up, near), (down, near))
    return jnp.stack([base + t for base, places in holders for t in places])


def halo_pieces(block):
    own = jnp.stack([from_before(block, "gz"), block, from_after(block, "gz")])
    outer = outer_swap(own)
    before, after = from_before(own, "gy"), from_after(own, "gy")
    inner = inner_swap(own)
    outer_before, outer_after = from_before(outer, "gy"), from_after(outer, "gy")
    inner_before, inner_after = inner_swap(before), inner_swap(after)
    return (
        own, before, after,
        outer, outer_before, outer_after,
        inner, inner_before, inner_after,
    )


def off_chip(x):
    return pltpu.with_memory_space_constraint(x, pltpu.HBM)


def whole_blocks(count):
    return [pl.BlockSpec(memory_space=pltpu.VMEM)] * count


def picked(index, rows):
    count = index.shape[1]
    wide = lax.transpose(jnp.broadcast_to(index, (rows, count)), (1, 0))
    lane = lax.broadcasted_iota(jnp.int32, (count, rows), 1)
    return jnp.where(wide == lane, 1.0, 0.0).astype(jnp.bfloat16)


def boundary_kernel(index_ref, rows_ref, out_ref):
    hit = picked(index_ref[...], rows_ref.shape[0])
    out_ref[...] = jnp.dot(hit, rows_ref[...], preferred_element_type=jnp.float32).astype(
        out_ref.dtype
    )


def boundary_of(index, rows):
    return pl.pallas_call(
        boundary_kernel,
        in_specs=whole_blocks(2),
        out_specs=pl.BlockSpec(memory_space=pltpu.VMEM),
        out_shape=jax.ShapeDtypeStruct((index.shape[1], rows.shape[1]), rows.dtype),
        compiler_params=pltpu.CompilerParams(vmem_limit_bytes=SMALL_BYTES),
        name="boundary",
    )(index, rows)


def whole_part(value, divisor):
    return jnp.floor((value.astype(jnp.float32) + 0.5) * (1.0 / divisor)).astype(jnp.int32)


def table_row(source, atoms, halo_count, odd):
    outside = jnp.maximum(source - atoms, 0)
    k = whole_part(outside, halo_count)
    row = outside - k * halo_count
    cell = jnp.where(k >= 13, k + 1, k)
    a = whole_part(cell, 9)
    b = whole_part(cell, 3) - 3 * a
    c = cell - 9 * a - 3 * b
    column = jnp.where(a == 1, 0, jnp.where(a == 2 * odd, 1, 2))
    turn = jnp.where(b == 1, 0, jnp.where(b == 0, 1, 2))
    there = atoms + ((column * 3 + turn) * 3 + c) * halo_count + row
    return jnp.where(source < atoms, source, there)


def gather_kernel(halo_count, order_ref, count_ref, source_hbm, target_hbm, basis_ref, *refs):
    table, slots_ref, picks, source_ref, target_ref, early, sems, out_sems = refs[-8:]
    parts, outs = refs[: -8 - slots_ref.shape[0]], refs[-8 - slots_ref.shape[0] : -8]
    slots = source_ref.shape[1]
    indices = [
        pltpu.make_async_copy(here, there, early.at[n])
        for n, (here, there) in enumerate(((source_hbm, source_ref), (target_hbm, target_ref)))
    ]
    for copy in indices:
        copy.start()
    atoms, width = parts[0].shape
    radial = basis_ref.shape[2]
    start = 0
    copies = []
    for n, part in enumerate(parts):
        there = table.at[pl.ds(start, part.shape[0])]
        copies.append(pltpu.make_async_copy(part, there, sems.at[n]))
        start += part.shape[0]
    for g in range(2 * len(outs)):
        there = slots_ref.at[g // 2, pl.ds(g % 2 * slots, slots), pl.ds(width, radial)]
        copies.append(
            pltpu.make_async_copy(basis_ref.at[order_ref[g]], there, sems.at[len(parts) + g])
        )
    for copy in copies:
        copy.start()
    table[start:] = jnp.zeros((table.shape[0] - start, width), table.dtype)
    for copy in indices:
        copy.wait()
    lane = lax.broadcasted_iota(jnp.int32, (slots, 128), 1)
    slot = lax.broadcasted_iota(jnp.int32, (1, slots), 1)
    line = lax.broadcasted_iota(jnp.int32, (16, slots), 0)
    end = 2 * slots
    sent = []
    for g, out_ref in enumerate(outs):
        ends = jnp.zeros((16, slots), jnp.float32)
        for t in range(2):
            j = order_ref[2 * g + t]
            row = table_row(source_ref[pl.ds(j, 1)], atoms, halo_count, order_ref[2 * len(outs)])
            wide = lax.transpose(jnp.broadcast_to(row, (128, slots)), (1, 0))
            spot = jnp.where((wide & 127) == lane, 1.0, 0.0).astype(jnp.bfloat16)
            tile = (wide >> 7).astype(jnp.float32).astype(jnp.bfloat16)
            for n in range(table.shape[0] // 128):
                here = tile == jnp.full((), n, jnp.bfloat16)
                picks[t * slots : (t + 1) * slots, n * 128 : (n + 1) * 128] = jnp.where(
                    here, spot, jnp.zeros_like(spot)
                )
            target = jnp.where(slot < count_ref[j], target_ref[pl.ds(j, 1)], -1)
            ends = jnp.where(line == t, target.astype(jnp.float32), ends)
        if g == 0:
            for copy in copies:
                copy.wait()
        slots_ref[g, :end, :width] = jnp.dot(
            picks[...], table[...], preferred_element_type=jnp.float32
        ).astype(table.dtype)
        slots_ref[g, end : end + atoms, :width] = table[:atoms]
        slots_ref[g, end : end + atoms, width:] = jnp.zeros((atoms, radial), table.dtype)
        slots_ref[g, end + atoms :, :slots] = ends.astype(table.dtype)
        slots_ref[g, end + atoms :, slots:] = jnp.zeros((16, width + radial - slots), table.dtype)
        copy = pltpu.make_async_copy(slots_ref.at[g], out_ref, out_sems.at[g])
        copy.start()
        sent.append(copy)
    for copy in sent:
        copy.wait()


def gather_rows(order, count, source, target, basis, parts, halo_count):
    slots = source.shape[1]
    atoms, width = parts[0].shape
    radial = basis.shape[2]
    rows = -(-sum(part.shape[0] for part in parts) // 256) * 256
    dtype = parts[0].dtype
    holders = (order.shape[0] - 1) // 2
    shape = (2 * slots + atoms + 16, width + radial)
    anywhere = pl.BlockSpec(memory_space=pl.ANY)
    return pl.pallas_call(
        functools.partial(gather_kernel, halo_count),
        in_specs=[pl.BlockSpec(memory_space=pltpu.SMEM)] * 2
        + [anywhere] * (3 + len(parts)),
        out_specs=[anywhere] * holders,
        out_shape=[jax.ShapeDtypeStruct(shape, dtype)] * holders,
        scratch_shapes=[
            pltpu.VMEM((rows, width), dtype),
            pltpu.VMEM((holders, *shape), dtype),
            pltpu.VMEM((2 * slots, rows), dtype),
            pltpu.VMEM(source.shape, source.dtype),
            pltpu.VMEM(target.shape, target.dtype),
            pltpu.SemaphoreType.DMA((2,)),
            pltpu.SemaphoreType.DMA((len(parts) + 2 * holders,)),
            pltpu.SemaphoreType.DMA((holders,)),
        ],
        compiler_params=pltpu.CompilerParams(vmem_limit_bytes=GATHER_BYTES),
        cost_estimate=pl.CostEstimate(
            flops=4 * holders * slots * rows * width,
            bytes_accessed=2 * width * (rows + 2 * holders * slots),
            transcendentals=0,
        ),
        name="source_rows",
    )(order, count, source, target, basis, *parts)


def half_parts(half, w_in, w_out, packed):
    depth, hidden = w_in.shape[0] // 2, w_in.shape[1]
    width = w_out.shape[1]
    rows = pl.ds(pl.multiple_of(half * depth, 16), depth)
    parts = []
    for n in range(hidden // width):
        there = packed.at[pl.ds(n * depth, depth)]
        parts.append((w_in.at[rows, pl.ds(n * width, width)], there))
    rows = pl.ds(pl.multiple_of(half * (hidden // 2), 16), hidden // 2)
    parts.append((w_out.at[rows], packed.at[pl.ds(hidden // width * depth, hidden // 2)]))
    return parts


def pack_kernel(half_ref, in_hbm, out_hbm, packed_ref, packed, sems, out_sems):
    first, second = [], []
    pairs = half_parts(half_ref[0], in_hbm.at[0], out_hbm.at[0], packed)
    ends = half_parts(0, in_hbm.at[0], out_hbm.at[0], packed_ref)
    for n, ((source, middle), (_, there)) in enumerate(zip(pairs, ends)):
        first.append(pltpu.make_async_copy(source, middle, sems.at[n]))
        second.append(pltpu.make_async_copy(middle, there, out_sems.at[n]))
    for copy in first:
        copy.start()
    for copy, onward in zip(first, second):
        copy.wait()
        onward.start()
    for copy in second:
        copy.wait()


def packed_half(half, w_in, w_out):
    depth, hidden, width = w_in.shape[1], w_out.shape[1], w_out.shape[2]
    shape = (depth // 2 * (hidden // width) + hidden // 2, width)
    outside = pl.BlockSpec(memory_space=pltpu.HBM)
    return pl.pallas_call(
        pack_kernel,
        in_specs=[pl.BlockSpec(memory_space=pltpu.SMEM)] + [outside] * 2,
        out_specs=outside,
        out_shape=jax.ShapeDtypeStruct(shape, w_in.dtype),
        scratch_shapes=[pltpu.VMEM(shape, w_in.dtype)]
        + [pltpu.SemaphoreType.DMA((1 + hidden // width,))] * 2,
        compiler_params=pltpu.CompilerParams(vmem_limit_bytes=SMALL_BYTES),
        name="packed_half",
    )(half, w_in, w_out)


def one_network(n, rows_ref, w_in, w_out, inputs, atoms):
    slots = inputs.shape[0]
    width = w_out.shape[1]
    start = 2 * slots
    target = rows_ref[start + atoms + n : start + atoms + n + 1, :slots].astype(jnp.float32)
    atom = lax.broadcasted_iota(jnp.int32, (atoms, slots), 0).astype(jnp.float32)
    incidence = jnp.where(atom == target, 1.0, 0.0)
    edges = slice(n * slots, (n + 1) * slots)
    inputs[:, :width] = rows_ref[edges, :width]
    inputs[:, width : 2 * width] = jnp.dot(
        lax.transpose(incidence, (1, 0)).astype(jnp.bfloat16),
        rows_ref[start : start + atoms, :width],
        preferred_element_type=jnp.float32,
    ).astype(jnp.bfloat16)
    inputs[:, 2 * width :] = rows_ref[edges, width:]
    pre = jnp.dot(inputs[...], w_in[...], preferred_element_type=jnp.float32)
    half = 0.5 * pre
    hidden = (half + half * jnp.tanh(half)).astype(jnp.bfloat16)
    message = jnp.dot(hidden, w_out[...], preferred_element_type=jnp.float32)
    return jnp.dot(
        incidence.astype(jnp.bfloat16),
        message.astype(jnp.bfloat16),
        preferred_element_type=jnp.float32,
    )


def first_kernel(half_ref, rows_hbm, in_0, out_0, here, there, *refs):
    in_ref, out_ref, sum_ref, rows_ref, inputs, sems = refs
    atoms = sum_ref.shape[0]
    pairs = [
        (rows_hbm, rows_ref),
        (in_0.at[0], in_ref.at[0]),
        (out_0.at[0], out_ref.at[0]),
    ]
    for half, packed in ((half_ref[0], here), (1 - half_ref[0], there)):
        pairs += [(b, a) for a, b in half_parts(half, in_ref.at[1], out_ref.at[1], packed)]
    copies = [
        pltpu.make_async_copy(source, end, sems.at[n]) for n, (source, end) in enumerate(pairs)
    ]
    for copy in copies:
        copy.start()
    for copy in copies[:3]:
        copy.wait()
    total = one_network(0, rows_ref, in_ref.at[0], out_ref.at[0], inputs, atoms)
    for copy in copies[3:]:
        copy.wait()
    sum_ref[...] = total + one_network(1, rows_ref, in_ref.at[1], out_ref.at[1], inputs, atoms)


def first_network(half, rows, atoms, mine, halves):
    width = mine[1].shape[2]
    slots = (rows.shape[0] - 16 - atoms) // 2
    outside = pl.BlockSpec(memory_space=pltpu.HBM)
    anywhere = pl.BlockSpec(memory_space=pl.ANY)
    shapes = [jax.ShapeDtypeStruct((2, *w.shape[1:]), w.dtype) for w in mine]
    return pl.pallas_call(
        first_kernel,
        in_specs=[pl.BlockSpec(memory_space=pltpu.SMEM), anywhere]
        + [outside] * 2
        + [anywhere] * 2,
        out_specs=whole_blocks(3),
        out_shape=[*shapes, jax.ShapeDtypeStruct((atoms, width), jnp.float32)],
        scratch_shapes=[
            pltpu.VMEM(rows.shape, rows.dtype),
            pltpu.VMEM((slots, mine[0].shape[1]), rows.dtype),
            pltpu.SemaphoreType.DMA((12,)),
        ],
        compiler_params=pltpu.CompilerParams(vmem_limit_bytes=FIRST_BYTES),
        name="own_network",
    )(half, rows, *mine, *halves)


def edge_kernel(rows_ref, w_in, w_out, sum_ref, inputs):
    atoms = sum_ref.shape[0]
    total = one_network(0, rows_ref, w_in.at[0], w_out.at[0], inputs, atoms)
    total += one_network(1, rows_ref, w_in.at[1], w_out.at[1], inputs, atoms)
    sum_ref[...] = total.astype(sum_ref.dtype)


def edge_network(rows, atoms, weights):
    w_in, w_out = weights
    width, hidden = w_out.shape[2], w_out.shape[1]
    slots = (rows.shape[0] - 16 - atoms) // 2
    return pl.pallas_call(
        edge_kernel,
        in_specs=whole_blocks(3),
        out_specs=pl.BlockSpec(memory_space=pltpu.VMEM),
        out_shape=jax.ShapeDtypeStruct((atoms, width), rows.dtype),
        scratch_shapes=[pltpu.VMEM((slots, w_in.shape[1]), rows.dtype)],
        compiler_params=pltpu.CompilerParams(vmem_limit_bytes=VMEM_BYTES),
        cost_estimate=pl.CostEstimate(
            flops=4 * slots * hidden * (w_in.shape[1] + width),
            bytes_accessed=2 * (rows.size + w_in.size + w_out.size),
            transcendentals=2 * slots * hidden,
        ),
        name="edge_network",
    )(rows, w_in, w_out)


def place_kernel(odd_ref, *refs):
    pieces, (out_ref, sems) = refs[:PIECES], refs[PIECES:]
    low = 17 * odd_ref[0]
    copies = []
    for n, piece in enumerate(pieces):
        column, turn = divmod(n, 3)
        b = (1, 0, 2)[turn]
        if n == 0:
            for c in (0, 2):
                copies.append((piece.at[pl.ds(c, 1)], out_ref.at[pl.ds(12 + c // 2, 1)]))
        else:
            if column == 0:
                start = 9 if b == 0 else 14
            else:
                start = 3 * b + (low if column == 1 else 17 - low)
            copies.append((piece, out_ref.at[pl.ds(start, 3)]))
    copies = [
        pltpu.make_async_copy(here, there, sems.at[i]) for i, (here, there) in enumerate(copies)
    ]
    for copy in copies:
        copy.start()
    for copy in copies:
        copy.wait()


def placed(pieces, odd):
    shape = pieces[0].shape
    return pl.pallas_call(
        place_kernel,
        in_specs=[pl.BlockSpec(memory_space=pltpu.SMEM)]
        + whole_blocks(PIECES),
        out_specs=pl.BlockSpec(memory_space=pl.ANY),
        out_shape=jax.ShapeDtypeStruct((26, *shape[1:]), pieces[0].dtype),
        scratch_shapes=[pltpu.SemaphoreType.DMA((10,))],
        compiler_params=pltpu.CompilerParams(vmem_limit_bytes=SMALL_BYTES),
        name="place_blocks",
    )(odd[None], *pieces)


def update_kernel(index_ref, rows_ref, weight_ref, own_ref, *refs):
    answers, (new_ref, edge_ref) = refs[:-2], refs[-2:]
    total = own_ref[...]
    for answer in answers:
        total += answer[...].astype(jnp.float32)
    mean_square = jnp.mean(total * total, axis=-1, keepdims=True)
    normed = (total * lax.rsqrt(mean_square + 1e-05)).astype(jnp.bfloat16)
    update = jnp.dot(normed, weight_ref[...], preferred_element_type=jnp.float32)
    new_rows = (rows_ref[...].astype(jnp.float32) + update).astype(new_ref.dtype)
    new_ref[...] = new_rows
    hit = picked(index_ref[...], new_rows.shape[0])
    edge_ref[...] = jnp.dot(hit, new_rows, preferred_element_type=jnp.float32).astype(
        edge_ref.dtype
    )


def updated(index, rows, weight, own, answers):
    return pl.pallas_call(
        update_kernel,
        in_specs=whole_blocks(4 + len(answers)),
        out_specs=whole_blocks(2),
        out_shape=[
            jax.ShapeDtypeStruct(rows.shape, rows.dtype),
            jax.ShapeDtypeStruct((index.shape[1], rows.shape[1]), rows.dtype),
        ],
        compiler_params=pltpu.CompilerParams(vmem_limit_bytes=SMALL_BYTES),
        name="update",
    )(index, rows, weight, own, *answers)


def shards(
    features,
    halo_index,
    edge_src,
    edge_dst,
    edge_count,
    edge_basis,
    w_edge_in,
    w_edge_out,
    w_update,
):
    atoms, width = features.shape
    groups, slots = edge_src.shape
    halo_count = halo_index.shape[0]
    halo_row = halo_index[None, :]
    odd = (lax.axis_index("gx") % 2).astype(jnp.int32)
    order = type_order()

    pieces = halo_pieces(boundary_of(halo_row, features))
    mine = tuple(off_chip(w) for w in (w_edge_in, w_edge_out))
    half = ((lax.axis_index("gy") + odd) % 2).astype(jnp.int32)[None]
    packed, _ = lax.optimization_barrier((packed_half(half, *mine), pieces[0]))
    packed = device_permute(packed, x_other)
    halves = (packed, device_permute(packed, y_partner))

    parts = [features] + [off_chip(piece.reshape(-1, width)) for piece in pieces]
    sources, targets = off_chip(edge_src), off_chip(edge_dst)
    basis = off_chip(edge_basis.reshape(groups, slots, -1))

    def gathered(*holders):
        pairs = [order[2 * n + t] for n in holders for t in range(2)]
        which = jnp.stack([*pairs, odd])
        return gather_rows(which, edge_count, sources, targets, basis, parts, halo_count)

    near, side = gathered(1, 2)
    near, side = device_permute(near, z_partner), device_permute(side, x_partner)
    far, here = gathered(3, 0)
    far = device_permute(far, far_partner)
    *weights, own = first_network(half, here, atoms, mine, halves)
    there, partners = (near, side, far), (z_partner, x_partner, far_partner)
    answers = []
    for rows, partner in zip(there, partners):
        answers.append(device_permute(edge_network(rows, atoms, weights), partner))

    new_rows, boundary = updated(halo_row, features, w_update, own, answers)
    return new_rows, placed(halo_pieces(boundary), odd)


def solution(mesh):
    everywhere = ("gx", "gy", "gz")
    in_specs = (
        P(everywhere, None),
        P(everywhere),
        P(everywhere, None),
        P(everywhere, None),
        P(everywhere),
        P(everywhere, None),
        P("gz", None, None),
        P("gz", None, None),
        P(),
    )
    out_specs = (P(everywhere, None), P(everywhere, None, None))
    return jax.shard_map(shards, mesh=mesh, in_specs=in_specs, out_specs=out_specs, check_vma=False)
```

```python
import functools

import jax
import jax.numpy as jnp
from jax import lax
from jax.experimental import pallas as pl
from jax.experimental.pallas import tpu as pltpu
from jax.sharding import PartitionSpec as P

PIECES = 9
VMEM_BYTES = 12 * 1024 * 1024
GATHER_BYTES = 16 * 1024 * 1024
FIRST_BYTES = 14 * 1024 * 1024
SMALL_BYTES = 5 * 1024 * 1024


def ring(axis, step):
    count = lax.axis_size(axis)
    return [(i, (i + step) % count) for i in range(count)]


def from_before(x, axis):
    return lax.ppermute(x, axis, ring(axis, 1))


def from_after(x, axis):
    return lax.ppermute(x, axis, ring(axis, -1))


def inner_swap(x):
    count = lax.axis_size("gx")
    return lax.ppermute(x, "gx", [(i, i ^ 1) for i in range(count)])


def outer_swap(x):
    count = lax.axis_size("gx")
    pairs = [(i, (i + 1) % count if i % 2 else (i - 1) % count) for i in range(count)]
    return lax.ppermute(x, "gx", pairs)


def paired(place, count, side):
    return (place + (1 if place % 2 == side else -1)) % count


def device_permute(x, move):
    shape = [lax.axis_size(axis) for axis in ("gx", "gy", "gz")]
    along = shape[2] // 2
    pairs = []
    for source in range(shape[0] * shape[1] * shape[2]):
        gx, gy, gz = source // (shape[1] * shape[2]), source // shape[2] % shape[1], source % shape[2]
        there = move(gz % along, gy, gx // 2 * 2 + gz // along, gx % 2, along, shape[0])
        px, py, pz, core = there
        gx, gz = pz // 2 * 2 + core, pz % 2 * along + px
        pairs.append((source, (gx * shape[1] + py) * shape[2] + gz))
    return lax.ppermute(x, ("gx", "gy", "gz"), pairs)


def x_partner(x, y, z, core, count, depth):
    return paired(x, count, core), y, z, core


def z_partner(x, y, z, core, count, depth):
    return x, y, paired(z, depth, core), core


def far_partner(x, y, z, core, count, depth):
    return paired(x, count, core), y, paired(z, depth, core), core


def y_partner(x, y, z, core, count, depth):
    return x, paired(y, lax.axis_size("gy"), core), z, core


def x_other(x, y, z, core, count, depth):
    return paired(x, count, 1 - core), y, z, core


def type_order():
    count = lax.axis_size("gz") // 2
    core, gz = lax.axis_index("gx") % 2, lax.axis_index("gz")
    x, low = gz % count, gz // count

    def beside(place, side):
        return (place + jnp.where(place % 2 == side, 1, -1)) % count

    here = [x, beside(x, 1 - core)]
    near = [beside(x, core), beside(beside(x, core), 1 - core)]
    up, down = low * count, (1 - low) * count
    holders = ((up, here), (down, here), (up, near), (down, near))
    return jnp.stack([base + t for base, places in holders for t in places])


def halo_pieces(block):
    own = jnp.stack([from_before(block, "gz"), block, from_after(block, "gz")])
    outer = outer_swap(own)
    before, after = from_before(own, "gy"), from_after(own, "gy")
    inner = inner_swap(own)
    outer_before, outer_after = from_before(outer, "gy"), from_after(outer, "gy")
    inner_before, inner_after = inner_swap(before), inner_swap(after)
    return (
        own, before, after,
        outer, outer_before, outer_after,
        inner, inner_before, inner_after,
    )


def off_chip(x):
    return pltpu.with_memory_space_constraint(x, pltpu.HBM)


def whole_blocks(count):
    return [pl.BlockSpec(memory_space=pltpu.VMEM)] * count


def picked(index, rows):
    count = index.shape[1]
    wide = lax.transpose(jnp.broadcast_to(index, (rows, count)), (1, 0))
    lane = lax.broadcasted_iota(jnp.int32, (count, rows), 1)
    return jnp.where(wide == lane, 1.0, 0.0).astype(jnp.bfloat16)


def boundary_kernel(index_ref, rows_ref, out_ref):
    hit = picked(index_ref[...], rows_ref.shape[0])
    out_ref[...] = jnp.dot(hit, rows_ref[...], preferred_element_type=jnp.float32).astype(
        out_ref.dtype
    )


def boundary_of(index, rows):
    return pl.pallas_call(
        boundary_kernel,
        in_specs=whole_blocks(2),
        out_specs=pl.BlockSpec(memory_space=pltpu.VMEM),
        out_shape=jax.ShapeDtypeStruct((index.shape[1], rows.shape[1]), rows.dtype),
        compiler_params=pltpu.CompilerParams(vmem_limit_bytes=SMALL_BYTES),
        name="boundary",
    )(index, rows)


def whole_part(value, divisor):
    return jnp.floor((value.astype(jnp.float32) + 0.5) * (1.0 / divisor)).astype(jnp.int32)


def table_row(source, atoms, halo_count, odd):
    outside = jnp.maximum(source - atoms, 0)
    k = whole_part(outside, halo_count)
    row = outside - k * halo_count
    cell = jnp.where(k >= 13, k + 1, k)
    a = whole_part(cell, 9)
    b = whole_part(cell, 3) - 3 * a
    c = cell - 9 * a - 3 * b
    column = jnp.where(a == 1, 0, jnp.where(a == 2 * odd, 1, 2))
    turn = jnp.where(b == 1, 0, jnp.where(b == 0, 1, 2))
    there = atoms + ((column * 3 + turn) * 3 + c) * halo_count + row
    return jnp.where(source < atoms, source, there)


def gather_kernel(halo_count, order_ref, count_ref, source_hbm, target_hbm, basis_ref, *refs):
    table, slots_ref, picks, source_ref, target_ref, early, sems, out_sems = refs[-8:]
    parts, outs = refs[: -8 - slots_ref.shape[0]], refs[-8 - slots_ref.shape[0] : -8]
    slots = source_ref.shape[1]
    indices = [
        pltpu.make_async_copy(here, there, early.at[n])
        for n, (here, there) in enumerate(((source_hbm, source_ref), (target_hbm, target_ref)))
    ]
    for copy in indices:
        copy.start()
    atoms, width = parts[0].shape
    radial = basis_ref.shape[2]
    start = 0
    copies = []
    for n, part in enumerate(parts):
        there = table.at[pl.ds(start, part.shape[0])]
        copies.append(pltpu.make_async_copy(part, there, sems.at[n]))
        start += part.shape[0]
    for g in range(2 * len(outs)):
        there = slots_ref.at[g // 2, pl.ds(g % 2 * slots, slots), pl.ds(width, radial)]
        copies.append(
            pltpu.make_async_copy(basis_ref.at[order_ref[g]], there, sems.at[len(parts) + g])
        )
    for copy in copies:
        copy.start()
    table[start:] = jnp.zeros((table.shape[0] - start, width), table.dtype)
    for copy in indices:
        copy.wait()
    lane = lax.broadcasted_iota(jnp.int32, (slots, 128), 1)
    slot = lax.broadcasted_iota(jnp.int32, (1, slots), 1)
    line = lax.broadcasted_iota(jnp.int32, (16, slots), 0)
    end = 2 * slots
    sent = [
        pltpu.make_async_copy(slots_ref.at[g], out_ref, out_sems.at[g])
        for g, out_ref in enumerate(outs)
    ]

    def one(g, carry):
        ends = jnp.zeros((16, slots), jnp.float32)
        for t in range(2):
            j = order_ref[2 * g + t]
            row = table_row(source_ref[pl.ds(j, 1)], atoms, halo_count, order_ref[2 * len(outs)])
            wide = lax.transpose(jnp.broadcast_to(row, (128, slots)), (1, 0))
            spot = jnp.where((wide & 127) == lane, 1.0, 0.0).astype(jnp.bfloat16)
            tile = (wide >> 7).astype(jnp.float32).astype(jnp.bfloat16)
            for n in range(table.shape[0] // 128):
                here = tile == jnp.full((), n, jnp.bfloat16)
                picks[t * slots : (t + 1) * slots, n * 128 : (n + 1) * 128] = jnp.where(
                    here, spot, jnp.zeros_like(spot)
                )
            target = jnp.where(slot < count_ref[j], target_ref[pl.ds(j, 1)], -1)
            ends = jnp.where(line == t, target.astype(jnp.float32), ends)

        @pl.when(g == 0)
        def _():
            for copy in copies:
                copy.wait()

        slots_ref[g, :end, :width] = jnp.dot(
            picks[...], table[...], preferred_element_type=jnp.float32
        ).astype(table.dtype)
        slots_ref[g, end : end + atoms, :width] = table[:atoms]
        slots_ref[g, end : end + atoms, width:] = jnp.zeros((atoms, radial), table.dtype)
        slots_ref[g, end + atoms :, :slots] = ends.astype(table.dtype)
        slots_ref[g, end + atoms :, slots:] = jnp.zeros((16, width + radial - slots), table.dtype)
        for n, copy in enumerate(sent):
            pl.when(g == n)(copy.start)
        return carry

    lax.fori_loop(0, len(outs), one, 0)
    for copy in sent:
        copy.wait()


def gather_rows(order, count, source, target, basis, parts, halo_count):
    slots = source.shape[1]
    atoms, width = parts[0].shape
    radial = basis.shape[2]
    rows = -(-sum(part.shape[0] for part in parts) // 256) * 256
    dtype = parts[0].dtype
    holders = (order.shape[0] - 1) // 2
    shape = (2 * slots + atoms + 16, width + radial)
    anywhere = pl.BlockSpec(memory_space=pl.ANY)
    return pl.pallas_call(
        functools.partial(gather_kernel, halo_count),
        in_specs=[pl.BlockSpec(memory_space=pltpu.SMEM)] * 2
        + [anywhere] * (3 + len(parts)),
        out_specs=[anywhere] * holders,
        out_shape=[jax.ShapeDtypeStruct(shape, dtype)] * holders,
        scratch_shapes=[
            pltpu.VMEM((rows, width), dtype),
            pltpu.VMEM((holders, *shape), dtype),
            pltpu.VMEM((2 * slots, rows), dtype),
            pltpu.VMEM(source.shape, source.dtype),
            pltpu.VMEM(target.shape, target.dtype),
            pltpu.SemaphoreType.DMA((2,)),
            pltpu.SemaphoreType.DMA((len(parts) + 2 * holders,)),
            pltpu.SemaphoreType.DMA((holders,)),
        ],
        compiler_params=pltpu.CompilerParams(vmem_limit_bytes=GATHER_BYTES),
        cost_estimate=pl.CostEstimate(
            flops=4 * holders * slots * rows * width,
            bytes_accessed=2 * width * (rows + 2 * holders * slots),
            transcendentals=0,
        ),
        name="source_rows",
    )(order, count, source, target, basis, *parts)


def half_parts(half, w_in, w_out, packed):
    depth, hidden = w_in.shape[0] // 2, w_in.shape[1]
    width = w_out.shape[1]
    rows = pl.ds(pl.multiple_of(half * depth, 16), depth)
    parts = []
    for n in range(hidden // width):
        there = packed.at[pl.ds(n * depth, depth)]
        parts.append((w_in.at[rows, pl.ds(n * width, width)], there))
    rows = pl.ds(pl.multiple_of(half * (hidden // 2), 16), hidden // 2)
    parts.append((w_out.at[rows], packed.at[pl.ds(hidden // width * depth, hidden // 2)]))
    return parts


def pack_kernel(half_ref, in_hbm, out_hbm, packed_ref, packed, sems, out_sems):
    first, second = [], []
    pairs = half_parts(half_ref[0], in_hbm.at[0], out_hbm.at[0], packed)
    ends = half_parts(0, in_hbm.at[0], out_hbm.at[0], packed_ref)
    for n, ((source, middle), (_, there)) in enumerate(zip(pairs, ends)):
        first.append(pltpu.make_async_copy(source, middle, sems.at[n]))
        second.append(pltpu.make_async_copy(middle, there, out_sems.at[n]))
    for copy in first:
        copy.start()
    for copy, onward in zip(first, second):
        copy.wait()
        onward.start()
    for copy in second:
        copy.wait()


def packed_half(half, w_in, w_out):
    depth, hidden, width = w_in.shape[1], w_out.shape[1], w_out.shape[2]
    shape = (depth // 2 * (hidden // width) + hidden // 2, width)
    outside = pl.BlockSpec(memory_space=pltpu.HBM)
    return pl.pallas_call(
        pack_kernel,
        in_specs=[pl.BlockSpec(memory_space=pltpu.SMEM)] + [outside] * 2,
        out_specs=outside,
        out_shape=jax.ShapeDtypeStruct(shape, w_in.dtype),
        scratch_shapes=[pltpu.VMEM(shape, w_in.dtype)]
        + [pltpu.SemaphoreType.DMA((1 + hidden // width,))] * 2,
        compiler_params=pltpu.CompilerParams(vmem_limit_bytes=SMALL_BYTES),
        name="packed_half",
    )(half, w_in, w_out)


def one_network(n, rows_ref, w_in, w_out, inputs, atoms):
    slots = inputs.shape[0]
    width = w_out.shape[1]
    start = 2 * slots
    target = rows_ref[start + atoms + n : start + atoms + n + 1, :slots].astype(jnp.float32)
    atom = lax.broadcasted_iota(jnp.int32, (atoms, slots), 0).astype(jnp.float32)
    incidence = jnp.where(atom == target, 1.0, 0.0)
    edges = slice(n * slots, (n + 1) * slots)
    inputs[:, :width] = rows_ref[edges, :width]
    inputs[:, width : 2 * width] = jnp.dot(
        lax.transpose(incidence, (1, 0)).astype(jnp.bfloat16),
        rows_ref[start : start + atoms, :width],
        preferred_element_type=jnp.float32,
    ).astype(jnp.bfloat16)
    inputs[:, 2 * width :] = rows_ref[edges, width:]
    pre = jnp.dot(inputs[...], w_in[...], preferred_element_type=jnp.float32)
    half = 0.5 * pre
    hidden = (half + half * jnp.tanh(half)).astype(jnp.bfloat16)
    message = jnp.dot(hidden, w_out[...], preferred_element_type=jnp.float32)
    return jnp.dot(
        incidence.astype(jnp.bfloat16),
        message.astype(jnp.bfloat16),
        preferred_element_type=jnp.float32,
    )


def first_kernel(half_ref, rows_hbm, in_0, out_0, here, there, *refs):
    in_ref, out_ref, sum_ref, rows_ref, inputs, sems = refs
    atoms = sum_ref.shape[0]
    pairs = [
        (rows_hbm, rows_ref),
        (in_0.at[0], in_ref.at[0]),
        (out_0.at[0], out_ref.at[0]),
    ]
    for half, packed in ((half_ref[0], here), (1 - half_ref[0], there)):
        pairs += [(b, a) for a, b in half_parts(half, in_ref.at[1], out_ref.at[1], packed)]
    copies = [
        pltpu.make_async_copy(source, end, sems.at[n]) for n, (source, end) in enumerate(pairs)
    ]
    for copy in copies:
        copy.start()
    for copy in copies[:3]:
        copy.wait()
    total = one_network(0, rows_ref, in_ref.at[0], out_ref.at[0], inputs, atoms)
    for copy in copies[3:]:
        copy.wait()
    sum_ref[...] = total + one_network(1, rows_ref, in_ref.at[1], out_ref.at[1], inputs, atoms)


def first_network(half, rows, atoms, mine, halves):
    width = mine[1].shape[2]
    slots = (rows.shape[0] - 16 - atoms) // 2
    outside = pl.BlockSpec(memory_space=pltpu.HBM)
    anywhere = pl.BlockSpec(memory_space=pl.ANY)
    shapes = [jax.ShapeDtypeStruct((2, *w.shape[1:]), w.dtype) for w in mine]
    return pl.pallas_call(
        first_kernel,
        in_specs=[pl.BlockSpec(memory_space=pltpu.SMEM), anywhere]
        + [outside] * 2
        + [anywhere] * 2,
        out_specs=whole_blocks(3),
        out_shape=[*shapes, jax.ShapeDtypeStruct((atoms, width), jnp.float32)],
        scratch_shapes=[
            pltpu.VMEM(rows.shape, rows.dtype),
            pltpu.VMEM((slots, mine[0].shape[1]), rows.dtype),
            pltpu.SemaphoreType.DMA((12,)),
        ],
        compiler_params=pltpu.CompilerParams(vmem_limit_bytes=FIRST_BYTES),
        name="own_network",
    )(half, rows, *mine, *halves)


def edge_kernel(rows_ref, w_in, w_out, sum_ref, inputs):
    atoms = sum_ref.shape[0]
    total = one_network(0, rows_ref, w_in.at[0], w_out.at[0], inputs, atoms)
    total += one_network(1, rows_ref, w_in.at[1], w_out.at[1], inputs, atoms)
    sum_ref[...] = total.astype(sum_ref.dtype)


def edge_network(rows, atoms, weights):
    w_in, w_out = weights
    width, hidden = w_out.shape[2], w_out.shape[1]
    slots = (rows.shape[0] - 16 - atoms) // 2
    return pl.pallas_call(
        edge_kernel,
        in_specs=whole_blocks(3),
        out_specs=pl.BlockSpec(memory_space=pltpu.VMEM),
        out_shape=jax.ShapeDtypeStruct((atoms, width), rows.dtype),
        scratch_shapes=[pltpu.VMEM((slots, w_in.shape[1]), rows.dtype)],
        compiler_params=pltpu.CompilerParams(vmem_limit_bytes=VMEM_BYTES),
        cost_estimate=pl.CostEstimate(
            flops=4 * slots * hidden * (w_in.shape[1] + width),
            bytes_accessed=2 * (rows.size + w_in.size + w_out.size),
            transcendentals=2 * slots * hidden,
        ),
        name="edge_network",
    )(rows, w_in, w_out)


def place_kernel(odd_ref, *refs):
    pieces, (out_ref, sems) = refs[:PIECES], refs[PIECES:]
    low = 17 * odd_ref[0]
    copies = []
    for n, piece in enumerate(pieces):
        column, turn = divmod(n, 3)
        b = (1, 0, 2)[turn]
        if n == 0:
            for c in (0, 2):
                copies.append((piece.at[pl.ds(c, 1)], out_ref.at[pl.ds(12 + c // 2, 1)]))
        else:
            if column == 0:
                start = 9 if b == 0 else 14
            else:
                start = 3 * b + (low if column == 1 else 17 - low)
            copies.append((piece, out_ref.at[pl.ds(start, 3)]))
    copies = [
        pltpu.make_async_copy(here, there, sems.at[i]) for i, (here, there) in enumerate(copies)
    ]
    for copy in copies:
        copy.start()
    for copy in copies:
        copy.wait()


def placed(pieces, odd):
    shape = pieces[0].shape
    return pl.pallas_call(
        place_kernel,
        in_specs=[pl.BlockSpec(memory_space=pltpu.SMEM)]
        + whole_blocks(PIECES),
        out_specs=pl.BlockSpec(memory_space=pl.ANY),
        out_shape=jax.ShapeDtypeStruct((26, *shape[1:]), pieces[0].dtype),
        scratch_shapes=[pltpu.SemaphoreType.DMA((10,))],
        compiler_params=pltpu.CompilerParams(vmem_limit_bytes=SMALL_BYTES),
        name="place_blocks",
    )(odd[None], *pieces)


def update_kernel(index_ref, rows_ref, weight_ref, own_ref, *refs):
    answers, (new_ref, edge_ref) = refs[:-2], refs[-2:]
    total = own_ref[...]
    for answer in answers:
        total += answer[...].astype(jnp.float32)
    mean_square = jnp.mean(total * total, axis=-1, keepdims=True)
    normed = (total * lax.rsqrt(mean_square + 1e-05)).astype(jnp.bfloat16)
    update = jnp.dot(normed, weight_ref[...], preferred_element_type=jnp.float32)
    new_rows = (rows_ref[...].astype(jnp.float32) + update).astype(new_ref.dtype)
    new_ref[...] = new_rows
    hit = picked(index_ref[...], new_rows.shape[0])
    edge_ref[...] = jnp.dot(hit, new_rows, preferred_element_type=jnp.float32).astype(
        edge_ref.dtype
    )


def updated(index, rows, weight, own, answers):
    return pl.pallas_call(
        update_kernel,
        in_specs=whole_blocks(4 + len(answers)),
        out_specs=whole_blocks(2),
        out_shape=[
            jax.ShapeDtypeStruct(rows.shape, rows.dtype),
            jax.ShapeDtypeStruct((index.shape[1], rows.shape[1]), rows.dtype),
        ],
        compiler_params=pltpu.CompilerParams(vmem_limit_bytes=SMALL_BYTES),
        name="update",
    )(index, rows, weight, own, *answers)


def shards(
    features,
    halo_index,
    edge_src,
    edge_dst,
    edge_count,
    edge_basis,
    w_edge_in,
    w_edge_out,
    w_update,
):
    atoms, width = features.shape
    groups, slots = edge_src.shape
    halo_count = halo_index.shape[0]
    halo_row = halo_index[None, :]
    odd = (lax.axis_index("gx") % 2).astype(jnp.int32)
    order = type_order()

    boundary = boundary_of(halo_row, features)
    pieces = halo_pieces(boundary)
    mine = tuple(off_chip(w) for w in (w_edge_in, w_edge_out))
    half = ((lax.axis_index("gy") + odd) % 2).astype(jnp.int32)[None]
    packed, _ = lax.optimization_barrier((packed_half(half, *mine), pieces[0]))
    packed = device_permute(packed, x_other)
    halves = (packed, device_permute(packed, y_partner))

    parts = [features] + [off_chip(piece.reshape(-1, width)) for piece in pieces]
    sources, targets = off_chip(edge_src), off_chip(edge_dst)
    basis = off_chip(edge_basis.reshape(groups, slots, -1))

    def gathered(*holders):
        pairs = [order[2 * n + t] for n in holders for t in range(2)]
        which = jnp.stack([*pairs, odd])
        return gather_rows(which, edge_count, sources, targets, basis, parts, halo_count)

    near, side = gathered(1, 2)
    near, side = device_permute(near, z_partner), device_permute(side, x_partner)
    far, here = gathered(3, 0)
    far = device_permute(far, far_partner)
    *weights, own = first_network(half, here, atoms, mine, halves)
    there, partners = (near, side, far), (z_partner, x_partner, far_partner)
    answers = []
    for rows, partner in zip(there, partners):
        answers.append(device_permute(edge_network(rows, atoms, weights), partner))

    new_rows, boundary = updated(halo_row, features, w_update, own, answers)
    return new_rows, placed(halo_pieces(boundary), odd)


def solution(mesh):
    everywhere = ("gx", "gy", "gz")
    in_specs = (
        P(everywhere, None),
        P(everywhere),
        P(everywhere, None),
        P(everywhere, None),
        P(everywhere),
        P(everywhere, None),
        P("gz", None, None),
        P("gz", None, None),
        P(),
    )
    out_specs = (P(everywhere, None), P(everywhere, None, None))
    return jax.shard_map(shards, mesh=mesh, in_specs=in_specs, out_specs=out_specs, check_vma=False)
```

```python
import functools

import jax
import jax.numpy as jnp
from jax import lax
from jax.experimental import pallas as pl
from jax.experimental.pallas import tpu as pltpu
from jax.sharding import PartitionSpec as P

PIECES = 9
VMEM_BYTES = 12 * 1024 * 1024
GATHER_BYTES = 16 * 1024 * 1024
FIRST_BYTES = 14 * 1024 * 1024
SMALL_BYTES = 5 * 1024 * 1024


def ring(axis, step):
    count = lax.axis_size(axis)
    return [(i, (i + step) % count) for i in range(count)]


def from_before(x, axis):
    return lax.ppermute(x, axis, ring(axis, 1))


def from_after(x, axis):
    return lax.ppermute(x, axis, ring(axis, -1))


def inner_swap(x):
    count = lax.axis_size("gx")
    return lax.ppermute(x, "gx", [(i, i ^ 1) for i in range(count)])


def outer_swap(x):
    count = lax.axis_size("gx")
    pairs = [(i, (i + 1) % count if i % 2 else (i - 1) % count) for i in range(count)]
    return lax.ppermute(x, "gx", pairs)


def paired(place, count, side):
    return (place + (1 if place % 2 == side else -1)) % count


def device_permute(x, move):
    shape = [lax.axis_size(axis) for axis in ("gx", "gy", "gz")]
    along = shape[2] // 2
    pairs = []
    for source in range(shape[0] * shape[1] * shape[2]):
        gx, gy, gz = source // (shape[1] * shape[2]), source // shape[2] % shape[1], source % shape[2]
        there = move(gz % along, gy, gx // 2 * 2 + gz // along, gx % 2, along, shape[0])
        px, py, pz, core = there
        gx, gz = pz // 2 * 2 + core, pz % 2 * along + px
        pairs.append((source, (gx * shape[1] + py) * shape[2] + gz))
    return lax.ppermute(x, ("gx", "gy", "gz"), pairs)


def x_partner(x, y, z, core, count, depth):
    return paired(x, count, core), y, z, core


def z_partner(x, y, z, core, count, depth):
    return x, y, paired(z, depth, core), core


def far_partner(x, y, z, core, count, depth):
    return paired(x, count, core), y, paired(z, depth, core), core


def y_partner(x, y, z, core, count, depth):
    return x, paired(y, lax.axis_size("gy"), core), z, core


def x_other(x, y, z, core, count, depth):
    return paired(x, count, 1 - core), y, z, core


def type_order():
    count = lax.axis_size("gz") // 2
    core, gz = lax.axis_index("gx") % 2, lax.axis_index("gz")
    x, low = gz % count, gz // count

    def beside(place, side):
        return (place + jnp.where(place % 2 == side, 1, -1)) % count

    here = [x, beside(x, 1 - core)]
    near = [beside(x, core), beside(beside(x, core), 1 - core)]
    up, down = low * count, (1 - low) * count
    holders = ((up, here), (down, here), (up, near), (down, near))
    return jnp.stack([base + t for base, places in holders for t in places])


def halo_pieces(block):
    own = jnp.stack([from_before(block, "gz"), block, from_after(block, "gz")])
    outer = outer_swap(own)
    before, after = from_before(own, "gy"), from_after(own, "gy")
    inner = inner_swap(own)
    outer_before, outer_after = from_before(outer, "gy"), from_after(outer, "gy")
    inner_before, inner_after = inner_swap(before), inner_swap(after)
    return (
        own, before, after,
        outer, outer_before, outer_after,
        inner, inner_before, inner_after,
    )


def off_chip(x):
    return pltpu.with_memory_space_constraint(x, pltpu.HBM)


def whole_blocks(count):
    return [pl.BlockSpec(memory_space=pltpu.VMEM)] * count


def picked(index, rows):
    count = index.shape[1]
    wide = lax.transpose(jnp.broadcast_to(index, (rows, count)), (1, 0))
    lane = lax.broadcasted_iota(jnp.int32, (count, rows), 1)
    return jnp.where(wide == lane, 1.0, 0.0).astype(jnp.bfloat16)


def boundary_kernel(index_hbm, rows_hbm, out_ref, index_ref, rows_ref, sems):
    copies = [
        pltpu.make_async_copy(index_hbm, index_ref, sems.at[0]),
        pltpu.make_async_copy(rows_hbm, rows_ref, sems.at[1]),
    ]
    for copy in copies:
        copy.start()
    for copy in copies:
        copy.wait()
    hit = picked(index_ref[...], rows_ref.shape[0])
    out_ref[...] = jnp.dot(hit, rows_ref[...], preferred_element_type=jnp.float32).astype(
        out_ref.dtype
    )


def boundary_of(index, rows):
    return pl.pallas_call(
        boundary_kernel,
        in_specs=[pl.BlockSpec(memory_space=pltpu.HBM)] * 2,
        out_specs=pl.BlockSpec(memory_space=pltpu.VMEM),
        out_shape=jax.ShapeDtypeStruct((index.shape[1], rows.shape[1]), rows.dtype),
        scratch_shapes=[
            pltpu.VMEM(index.shape, index.dtype),
            pltpu.VMEM(rows.shape, rows.dtype),
            pltpu.SemaphoreType.DMA((2,)),
        ],
        compiler_params=pltpu.CompilerParams(vmem_limit_bytes=SMALL_BYTES),
        name="boundary",
    )(off_chip(index), off_chip(rows))


def whole_part(value, divisor):
    return jnp.floor((value.astype(jnp.float32) + 0.5) * (1.0 / divisor)).astype(jnp.int32)


def table_row(source, atoms, halo_count, odd):
    outside = jnp.maximum(source - atoms, 0)
    k = whole_part(outside, halo_count)
    row = outside - k * halo_count
    cell = jnp.where(k >= 13, k + 1, k)
    a = whole_part(cell, 9)
    b = whole_part(cell, 3) - 3 * a
    c = cell - 9 * a - 3 * b
    column = jnp.where(a == 1, 0, jnp.where(a == 2 * odd, 1, 2))
    turn = jnp.where(b == 1, 0, jnp.where(b == 0, 1, 2))
    there = atoms + ((column * 3 + turn) * 3 + c) * halo_count + row
    return jnp.where(source < atoms, source, there)


def gather_kernel(halo_count, order_ref, count_ref, source_hbm, target_hbm, basis_ref, *refs):
    table, slots_ref, picks, source_ref, target_ref, early, sems, out_sems = refs[-8:]
    parts, outs = refs[: -8 - slots_ref.shape[0]], refs[-8 - slots_ref.shape[0] : -8]
    slots = source_ref.shape[1]
    indices = [
        pltpu.make_async_copy(here, there, early.at[n])
        for n, (here, there) in enumerate(((source_hbm, source_ref), (target_hbm, target_ref)))
    ]
    for copy in indices:
        copy.start()
    atoms, width = parts[0].shape
    radial = basis_ref.shape[2]
    start = 0
    copies = []
    for n, part in enumerate(parts):
        there = table.at[pl.ds(start, part.shape[0])]
        copies.append(pltpu.make_async_copy(part, there, sems.at[n]))
        start += part.shape[0]
    for g in range(2 * len(outs)):
        there = slots_ref.at[g // 2, pl.ds(g % 2 * slots, slots), pl.ds(width, radial)]
        copies.append(
            pltpu.make_async_copy(basis_ref.at[order_ref[g]], there, sems.at[len(parts) + g])
        )
    for copy in copies:
        copy.start()
    table[start:] = jnp.zeros((table.shape[0] - start, width), table.dtype)
    for copy in indices:
        copy.wait()
    lane = lax.broadcasted_iota(jnp.int32, (slots, 128), 1)
    slot = lax.broadcasted_iota(jnp.int32, (1, slots), 1)
    line = lax.broadcasted_iota(jnp.int32, (16, slots), 0)
    end = 2 * slots
    sent = [
        pltpu.make_async_copy(slots_ref.at[g], out_ref, out_sems.at[g])
        for g, out_ref in enumerate(outs)
    ]

    def one(g, carry):
        ends = jnp.zeros((16, slots), jnp.float32)
        for t in range(2):
            j = order_ref[2 * g + t]
            row = table_row(source_ref[pl.ds(j, 1)], atoms, halo_count, order_ref[2 * len(outs)])
            wide = lax.transpose(jnp.broadcast_to(row, (128, slots)), (1, 0))
            spot = jnp.where((wide & 127) == lane, 1.0, 0.0).astype(jnp.bfloat16)
            tile = (wide >> 7).astype(jnp.float32).astype(jnp.bfloat16)
            for n in range(table.shape[0] // 128):
                here = tile == jnp.full((), n, jnp.bfloat16)
                picks[t * slots : (t + 1) * slots, n * 128 : (n + 1) * 128] = jnp.where(
                    here, spot, jnp.zeros_like(spot)
                )
            target = jnp.where(slot < count_ref[j], target_ref[pl.ds(j, 1)], -1)
            ends = jnp.where(line == t, target.astype(jnp.float32), ends)

        @pl.when(g == 0)
        def _():
            for copy in copies:
                copy.wait()

        slots_ref[g, :end, :width] = jnp.dot(
            picks[...], table[...], preferred_element_type=jnp.float32
        ).astype(table.dtype)
        slots_ref[g, end : end + atoms, :width] = table[:atoms]
        slots_ref[g, end : end + atoms, width:] = jnp.zeros((atoms, radial), table.dtype)
        slots_ref[g, end + atoms :, :slots] = ends.astype(table.dtype)
        slots_ref[g, end + atoms :, slots:] = jnp.zeros((16, width + radial - slots), table.dtype)
        for n, copy in enumerate(sent):
            pl.when(g == n)(copy.start)
        return carry

    lax.fori_loop(0, len(outs), one, 0)
    for copy in sent:
        copy.wait()


def gather_rows(order, count, source, target, basis, parts, halo_count):
    slots = source.shape[1]
    atoms, width = parts[0].shape
    radial = basis.shape[2]
    rows = -(-sum(part.shape[0] for part in parts) // 256) * 256
    dtype = parts[0].dtype
    holders = (order.shape[0] - 1) // 2
    shape = (2 * slots + atoms + 16, width + radial)
    anywhere = pl.BlockSpec(memory_space=pl.ANY)
    return pl.pallas_call(
        functools.partial(gather_kernel, halo_count),
        in_specs=[pl.BlockSpec(memory_space=pltpu.SMEM)] * 2
        + [anywhere] * (3 + len(parts)),
        out_specs=[anywhere] * holders,
        out_shape=[jax.ShapeDtypeStruct(shape, dtype)] * holders,
        scratch_shapes=[
            pltpu.VMEM((rows, width), dtype),
            pltpu.VMEM((holders, *shape), dtype),
            pltpu.VMEM((2 * slots, rows), dtype),
            pltpu.VMEM(source.shape, source.dtype),
            pltpu.VMEM(target.shape, target.dtype),
            pltpu.SemaphoreType.DMA((2,)),
            pltpu.SemaphoreType.DMA((len(parts) + 2 * holders,)),
            pltpu.SemaphoreType.DMA((holders,)),
        ],
        compiler_params=pltpu.CompilerParams(vmem_limit_bytes=GATHER_BYTES),
        cost_estimate=pl.CostEstimate(
            flops=4 * holders * slots * rows * width,
            bytes_accessed=2 * width * (rows + 2 * holders * slots),
            transcendentals=0,
        ),
        name="source_rows",
    )(order, count, source, target, basis, *parts)


def half_parts(half, w_in, w_out, packed):
    depth, hidden = w_in.shape[0] // 2, w_in.shape[1]
    width = w_out.shape[1]
    rows = pl.ds(pl.multiple_of(half * depth, 16), depth)
    parts = []
    for n in range(hidden // width):
        there = packed.at[pl.ds(n * depth, depth)]
        parts.append((w_in.at[rows, pl.ds(n * width, width)], there))
    rows = pl.ds(pl.multiple_of(half * (hidden // 2), 16), hidden // 2)
    parts.append((w_out.at[rows], packed.at[pl.ds(hidden // width * depth, hidden // 2)]))
    return parts


def pack_kernel(half_ref, in_hbm, out_hbm, packed_ref, packed, sems, out_sems):
    first, second = [], []
    pairs = half_parts(half_ref[0], in_hbm.at[0], out_hbm.at[0], packed)
    ends = half_parts(0, in_hbm.at[0], out_hbm.at[0], packed_ref)
    for n, ((source, middle), (_, there)) in enumerate(zip(pairs, ends)):
        first.append(pltpu.make_async_copy(source, middle, sems.at[n]))
        second.append(pltpu.make_async_copy(middle, there, out_sems.at[n]))
    for copy in first:
        copy.start()
    for copy, onward in zip(first, second):
        copy.wait()
        onward.start()
    for copy in second:
        copy.wait()


def packed_half(half, w_in, w_out):
    depth, hidden, width = w_in.shape[1], w_out.shape[1], w_out.shape[2]
    shape = (depth // 2 * (hidden // width) + hidden // 2, width)
    outside = pl.BlockSpec(memory_space=pltpu.HBM)
    return pl.pallas_call(
        pack_kernel,
        in_specs=[pl.BlockSpec(memory_space=pltpu.SMEM)] + [outside] * 2,
        out_specs=outside,
        out_shape=jax.ShapeDtypeStruct(shape, w_in.dtype),
        scratch_shapes=[pltpu.VMEM(shape, w_in.dtype)]
        + [pltpu.SemaphoreType.DMA((1 + hidden // width,))] * 2,
        compiler_params=pltpu.CompilerParams(vmem_limit_bytes=SMALL_BYTES),
        name="packed_half",
    )(half, w_in, w_out)


def one_network(n, rows_ref, w_in, w_out, inputs, atoms):
    slots = inputs.shape[0]
    width = w_out.shape[1]
    start = 2 * slots
    target = rows_ref[start + atoms + n : start + atoms + n + 1, :slots].astype(jnp.float32)
    atom = lax.broadcasted_iota(jnp.int32, (atoms, slots), 0).astype(jnp.float32)
    incidence = jnp.where(atom == target, 1.0, 0.0)
    edges = slice(n * slots, (n + 1) * slots)
    inputs[:, :width] = rows_ref[edges, :width]
    inputs[:, width : 2 * width] = jnp.dot(
        lax.transpose(incidence, (1, 0)).astype(jnp.bfloat16),
        rows_ref[start : start + atoms, :width],
        preferred_element_type=jnp.float32,
    ).astype(jnp.bfloat16)
    inputs[:, 2 * width :] = rows_ref[edges, width:]
    pre = jnp.dot(inputs[...], w_in[...], preferred_element_type=jnp.float32)
    half = 0.5 * pre
    hidden = (half + half * jnp.tanh(half)).astype(jnp.bfloat16)
    message = jnp.dot(hidden, w_out[...], preferred_element_type=jnp.float32)
    return jnp.dot(
        incidence.astype(jnp.bfloat16),
        message.astype(jnp.bfloat16),
        preferred_element_type=jnp.float32,
    )


def first_kernel(half_ref, rows_hbm, in_0, out_0, here, there, *refs):
    in_ref, out_ref, sum_ref, rows_ref, inputs, sems = refs
    atoms = sum_ref.shape[0]
    pairs = [
        (rows_hbm, rows_ref),
        (in_0.at[0], in_ref.at[0]),
        (out_0.at[0], out_ref.at[0]),
    ]
    for half, packed in ((half_ref[0], here), (1 - half_ref[0], there)):
        pairs += [(b, a) for a, b in half_parts(half, in_ref.at[1], out_ref.at[1], packed)]
    copies = [
        pltpu.make_async_copy(source, end, sems.at[n]) for n, (source, end) in enumerate(pairs)
    ]
    for copy in copies:
        copy.start()
    for copy in copies[:3]:
        copy.wait()
    total = one_network(0, rows_ref, in_ref.at[0], out_ref.at[0], inputs, atoms)
    for copy in copies[3:]:
        copy.wait()
    sum_ref[...] = total + one_network(1, rows_ref, in_ref.at[1], out_ref.at[1], inputs, atoms)


def first_network(half, rows, atoms, mine, halves):
    width = mine[1].shape[2]
    slots = (rows.shape[0] - 16 - atoms) // 2
    outside = pl.BlockSpec(memory_space=pltpu.HBM)
    anywhere = pl.BlockSpec(memory_space=pl.ANY)
    shapes = [jax.ShapeDtypeStruct((2, *w.shape[1:]), w.dtype) for w in mine]
    return pl.pallas_call(
        first_kernel,
        in_specs=[pl.BlockSpec(memory_space=pltpu.SMEM), anywhere]
        + [outside] * 2
        + [anywhere] * 2,
        out_specs=whole_blocks(3),
        out_shape=[*shapes, jax.ShapeDtypeStruct((atoms, width), jnp.float32)],
        scratch_shapes=[
            pltpu.VMEM(rows.shape, rows.dtype),
            pltpu.VMEM((slots, mine[0].shape[1]), rows.dtype),
            pltpu.SemaphoreType.DMA((12,)),
        ],
        compiler_params=pltpu.CompilerParams(vmem_limit_bytes=FIRST_BYTES),
        name="own_network",
    )(half, rows, *mine, *halves)


def edge_kernel(rows_ref, w_in, w_out, sum_ref, inputs):
    atoms = sum_ref.shape[0]
    total = one_network(0, rows_ref, w_in.at[0], w_out.at[0], inputs, atoms)
    total += one_network(1, rows_ref, w_in.at[1], w_out.at[1], inputs, atoms)
    sum_ref[...] = total.astype(sum_ref.dtype)


def edge_network(rows, atoms, weights):
    w_in, w_out = weights
    width, hidden = w_out.shape[2], w_out.shape[1]
    slots = (rows.shape[0] - 16 - atoms) // 2
    return pl.pallas_call(
        edge_kernel,
        in_specs=whole_blocks(3),
        out_specs=pl.BlockSpec(memory_space=pltpu.VMEM),
        out_shape=jax.ShapeDtypeStruct((atoms, width), rows.dtype),
        scratch_shapes=[pltpu.VMEM((slots, w_in.shape[1]), rows.dtype)],
        compiler_params=pltpu.CompilerParams(vmem_limit_bytes=VMEM_BYTES),
        cost_estimate=pl.CostEstimate(
            flops=4 * slots * hidden * (w_in.shape[1] + width),
            bytes_accessed=2 * (rows.size + w_in.size + w_out.size),
            transcendentals=2 * slots * hidden,
        ),
        name="edge_network",
    )(rows, w_in, w_out)


def place_kernel(odd_ref, *refs):
    pieces, (out_ref, sems) = refs[:PIECES], refs[PIECES:]
    low = 17 * odd_ref[0]
    copies = []
    for n, piece in enumerate(pieces):
        column, turn = divmod(n, 3)
        b = (1, 0, 2)[turn]
        if n == 0:
            for c in (0, 2):
                copies.append((piece.at[pl.ds(c, 1)], out_ref.at[pl.ds(12 + c // 2, 1)]))
        else:
            if column == 0:
                start = 9 if b == 0 else 14
            else:
                start = 3 * b + (low if column == 1 else 17 - low)
            copies.append((piece, out_ref.at[pl.ds(start, 3)]))
    copies = [
        pltpu.make_async_copy(here, there, sems.at[i]) for i, (here, there) in enumerate(copies)
    ]
    for copy in copies:
        copy.start()
    for copy in copies:
        copy.wait()


def placed(pieces, odd):
    shape = pieces[0].shape
    return pl.pallas_call(
        place_kernel,
        in_specs=[pl.BlockSpec(memory_space=pltpu.SMEM)]
        + whole_blocks(PIECES),
        out_specs=pl.BlockSpec(memory_space=pl.ANY),
        out_shape=jax.ShapeDtypeStruct((26, *shape[1:]), pieces[0].dtype),
        scratch_shapes=[pltpu.SemaphoreType.DMA((10,))],
        compiler_params=pltpu.CompilerParams(vmem_limit_bytes=SMALL_BYTES),
        name="place_blocks",
    )(odd[None], *pieces)


def update_kernel(index_ref, rows_ref, weight_ref, own_ref, *refs):
    answers, (new_ref, edge_ref) = refs[:-2], refs[-2:]
    total = own_ref[...]
    for answer in answers:
        total += answer[...].astype(jnp.float32)
    mean_square = jnp.mean(total * total, axis=-1, keepdims=True)
    normed = (total * lax.rsqrt(mean_square + 1e-05)).astype(jnp.bfloat16)
    update = jnp.dot(normed, weight_ref[...], preferred_element_type=jnp.float32)
    new_rows = (rows_ref[...].astype(jnp.float32) + update).astype(new_ref.dtype)
    new_ref[...] = new_rows
    hit = picked(index_ref[...], new_rows.shape[0])
    edge_ref[...] = jnp.dot(hit, new_rows, preferred_element_type=jnp.float32).astype(
        edge_ref.dtype
    )


def updated(index, rows, weight, own, answers):
    return pl.pallas_call(
        update_kernel,
        in_specs=whole_blocks(4 + len(answers)),
        out_specs=whole_blocks(2),
        out_shape=[
            jax.ShapeDtypeStruct(rows.shape, rows.dtype),
            jax.ShapeDtypeStruct((index.shape[1], rows.shape[1]), rows.dtype),
        ],
        compiler_params=pltpu.CompilerParams(vmem_limit_bytes=SMALL_BYTES),
        name="update",
    )(index, rows, weight, own, *answers)


def shards(
    features,
    halo_index,
    edge_src,
    edge_dst,
    edge_count,
    edge_basis,
    w_edge_in,
    w_edge_out,
    w_update,
):
    atoms, width = features.shape
    groups, slots = edge_src.shape
    halo_count = halo_index.shape[0]
    halo_row = halo_index[None, :]
    odd = (lax.axis_index("gx") % 2).astype(jnp.int32)
    order = type_order()

    boundary = boundary_of(halo_row, features)
    pieces = halo_pieces(boundary)
    mine = tuple(off_chip(w) for w in (w_edge_in, w_edge_out))
    half = ((lax.axis_index("gy") + odd) % 2).astype(jnp.int32)[None]
    packed, _ = lax.optimization_barrier((packed_half(half, *mine), pieces[0]))
    packed = device_permute(packed, x_other)
    halves = (packed, device_permute(packed, y_partner))

    parts = [features] + [off_chip(piece.reshape(-1, width)) for piece in pieces]
    sources, targets = off_chip(edge_src), off_chip(edge_dst)
    basis = off_chip(edge_basis.reshape(groups, slots, -1))

    def gathered(*holders):
        pairs = [order[2 * n + t] for n in holders for t in range(2)]
        which = jnp.stack([*pairs, odd])
        return gather_rows(which, edge_count, sources, targets, basis, parts, halo_count)

    near, side = gathered(1, 2)
    near, side = device_permute(near, z_partner), device_permute(side, x_partner)
    far, here = gathered(3, 0)
    far = device_permute(far, far_partner)
    *weights, own = first_network(half, here, atoms, mine, halves)
    there, partners = (near, side, far), (z_partner, x_partner, far_partner)
    answers = []
    for rows, partner in zip(there, partners):
        answers.append(device_permute(edge_network(rows, atoms, weights), partner))

    new_rows, boundary = updated(halo_row, features, w_update, own, answers)
    return new_rows, placed(halo_pieces(boundary), odd)


def solution(mesh):
    everywhere = ("gx", "gy", "gz")
    in_specs = (
        P(everywhere, None),
        P(everywhere),
        P(everywhere, None),
        P(everywhere, None),
        P(everywhere),
        P(everywhere, None),
        P("gz", None, None),
        P("gz", None, None),
        P(),
    )
    out_specs = (P(everywhere, None), P(everywhere, None, None))
    return jax.shard_map(shards, mesh=mesh, in_specs=in_specs, out_specs=out_specs, check_vma=False)
```
